128 devices in a mesh: outer: 8 (over x, core), inner: 16 (over z, y).
Axes of the slice: x: 4, y: 4, z: 4, core: 2. Of those that a mesh axis runs over, the one named last changes fastest.
Arguments:
- inputs: bfloat16 [512, 16, 16, 512], P(('outer', 'inner')), may hold values from -12 to 12
- cotangent: bfloat16 [512, 16, 16, 2048], P(('outer', 'inner')), may hold values from -12 to 12
- conv_weight: bfloat16 [4608, 512], replicated, may hold values from -1 to 1
- expand_weight: bfloat16 [512, 2048], replicated, may hold values from -2 to 2
- conv_momentum: float32 [128, 18432], P(('outer', 'inner')), may hold values from -6 to 6
- expand_momentum: float32 [128, 8192], P(('outer', 'inner')), may hold values from -6 to 6
Outputs:
- input_grad: bfloat16 [512, 16, 16, 512], P(('outer', 'inner'))
- conv_new: float32 [128, 18432], P(('outer', 'inner'))
- expand_new: float32 [128, 8192], P(('outer', 'inner'))
The draws below stay inside these ranges and needn't reach their ends.
All inputs are finite; a program needn't handle non-finite values.
Results may differ from the reference program's by a relative error of at most 0.01.
Values may be sent and summed in bfloat16 or wider, within the bound.
A program may use at most 128 MiB of HBM per device.

```python
import jax
import jax.numpy as jnp
from jax import lax

C = 512
E = 2048
H = 16
W = 16
IMG_DEV = 4
BATCH = 512
S2 = 18432
S3 = 8192
N_OUTER = 8
N_INNER = 16
DEVICES = 128


def mixed_field(key, shape, limit):
    k_common, k_group, k_weight, k_noise, k_scale = jax.random.split(key, 5)
    scales = jnp.exp(jax.random.uniform(k_scale, (shape[-1],), jnp.float32, jnp.log(0.3), jnp.log(3.0)))
    common = jax.random.normal(k_common, shape[1:], jnp.float32)
    group_fields = jax.random.normal(k_group, (N_OUTER,) + tuple(shape[1:]), jnp.float32)
    group_weight = jnp.exp(jax.random.uniform(k_weight, (N_OUTER,), jnp.float32, jnp.log(0.4), jnp.log(1.6)))
    owner = jnp.arange(shape[0]) // IMG_DEV // N_INNER
    own_field = group_fields[owner] * group_weight[owner][:, None, None, None]
    mixture = 0.45 * common + 0.75 * own_field + 0.5 * jax.random.normal(k_noise, shape, jnp.float32)
    return jnp.clip(mixture * scales, -limit, limit)


def channel_levels(key):
    block = C // N_OUTER
    place = (jnp.arange(C) % block).astype(jnp.float32) / block
    jitter = jnp.exp(jax.random.uniform(key, (C,), jnp.float32, jnp.log(0.7), jnp.log(1.4)))
    ratio = 2.2
    return (place, jitter * jnp.exp(jnp.log(ratio) * place))


def kernel_noise(key, shape):
    return jax.random.normal(key, shape, jnp.float32)


def draw_inputs(key, part):
    return mixed_field(jax.random.fold_in(key, 11), (BATCH, H, W, C), 12.0).astype(jnp.bfloat16)


def draw_cotangent(key, part):
    return mixed_field(jax.random.fold_in(key, 23), (BATCH, H, W, E), 12.0).astype(jnp.bfloat16)


def draw_conv_weight(key, part):
    k_noise, k_level = jax.random.split(jax.random.fold_in(key, 37))
    place, level = channel_levels(k_level)
    noise = kernel_noise(k_noise, (9 * C, C))
    kernel = noise * level[None, :] / jnp.sqrt(9.0 * C) + 3.0 * place[None, :] / (9.0 * C)
    return jnp.clip(kernel, -1.0, 1.0).astype(jnp.bfloat16)


def draw_expand_weight(key, part):
    k_noise, k_level = jax.random.split(jax.random.fold_in(key, 41))
    place, level = channel_levels(k_level)
    noise = kernel_noise(k_noise, (C, E))
    kernel = noise * level[:, None] / jnp.sqrt(1.0 * C)
    return jnp.clip(kernel, -2.0, 2.0).astype(jnp.bfloat16)


def levels(stream_key, shape, shards, smallest, top_value):
    loudness = 1.0
    for position, parts in shards:
        draws = jax.random.uniform(jax.random.fold_in(jax.random.fold_in(stream_key, 6), position), (parts,), jnp.float32, smallest / len(shards), top_value / len(shards))
        loudness = loudness * jnp.repeat(jnp.exp(draws), shape[position] // parts).reshape((-1,) + (1,) * (len(shape) - 1 - position))
    return loudness


def centred(rng, dims, deviation, bound, cuts=(), kind=jnp.bfloat16):
    entries = jax.random.normal(rng, dims, jnp.float32) * deviation
    if len(cuts) > 0:
        entries = levels(rng, dims, cuts, -0.22, 0.18) * entries
    return jnp.clip(entries, min=-bound, max=bound).astype(kind)


def setup_inputs(seed: int = 0) -> dict:
    streams_of = jax.random.split(jax.random.key(seed), 7)
    return {
        "inputs": draw_inputs(jax.random.fold_in(streams_of[6], 71), 0),
        "cotangent": draw_cotangent(jax.random.fold_in(streams_of[6], 71), 0),
        "conv_weight": draw_conv_weight(jax.random.fold_in(streams_of[6], 71), 0),
        "expand_weight": draw_expand_weight(jax.random.fold_in(streams_of[6], 71), 0),
        "conv_momentum": centred(streams_of[4], (DEVICES, S2), 1.0, 6.0, ((0, 128),), jnp.float32),
        "expand_momentum": centred(streams_of[5], (DEVICES, S3), 1.0, 6.0, ((0, 128),), jnp.float32),
    }


EPS = 1e-6
MOMENTUM = 0.9


def patches(image):
    images, height, across, channels = image.shape
    padded = jnp.pad(image, ((0, 0), (1, 1), (1, 1), (0, 0)))
    pieces = [padded[:, shift_y:shift_y + height, shift_x:shift_x + across, :] for shift_y in range(3) for shift_x in range(3)]
    return jnp.concatenate(pieces, axis=-1).reshape(images * height * across, 9 * channels)


def local_step(inputs, cotangent, conv_weight, expand_weight):
    images, height, across, channels = inputs.shape
    row_count = images * height * across
    relu_in = jnp.maximum(inputs, jnp.zeros((), inputs.dtype))
    columns = patches(relu_in)
    hidden_pre = jnp.dot(columns, conv_weight, preferred_element_type=jnp.float32).astype(jnp.bfloat16)
    hidden_act = jnp.maximum(hidden_pre, jnp.zeros((), hidden_pre.dtype))
    grad_rows = cotangent.reshape(row_count, cotangent.shape[-1])
    expand_grad = (lax.dot_general(hidden_act, grad_rows, (((0,), (0,)), ((), ())), preferred_element_type=jnp.float32) / row_count).astype(jnp.bfloat16)
    hidden_back = lax.dot_general(grad_rows, expand_weight, (((1,), (1,)), ((), ())), preferred_element_type=jnp.float32)
    hidden_grad = jnp.where(hidden_pre > 0, hidden_back, 0.0).astype(jnp.bfloat16)
    conv_grad = (lax.dot_general(columns, hidden_grad, (((0,), (0,)), ((), ())), preferred_element_type=jnp.float32) / row_count).astype(jnp.bfloat16)
    flipped = conv_weight.reshape(3, 3, channels, channels)[::-1, ::-1].transpose(0, 1, 3, 2).reshape(9 * channels, channels)
    back_cols = patches(hidden_grad.reshape(images, height, across, channels))
    input_back = jnp.dot(back_cols, flipped, preferred_element_type=jnp.float32)
    input_grad = jnp.where(inputs.reshape(row_count, channels) > 0, input_back, 0.0).astype(jnp.bfloat16)
    return input_grad.reshape(inputs.shape), conv_grad, expand_grad


def adasum_levels(vectors):
    outer_count = vectors.shape[0]
    group_span = 1
    while group_span < outer_count:
        grouped = vectors.reshape(outer_count // (2 * group_span), 2, group_span, vectors.shape[1])
        low_side = grouped[:, 0]
        high_side = grouped[:, 1]
        norm_low = jnp.sum(low_side * low_side, axis=-1, keepdims=True)
        norm_high = jnp.sum(high_side * high_side, axis=-1, keepdims=True)
        cross_dot = jnp.sum(low_side * high_side, axis=-1, keepdims=True)
        merged = (1.0 - cross_dot / (2.0 * (norm_low + EPS))) * low_side + (1.0 - cross_dot / (2.0 * (norm_high + EPS))) * high_side
        vectors = jnp.stack([merged, merged], axis=1).reshape(outer_count, vectors.shape[1])
        group_span = group_span * 2
    return vectors[0]


def reference(inputs, cotangent, conv_weight, expand_weight, conv_momentum, expand_momentum):
    device_inputs = inputs.reshape(N_OUTER, N_INNER, IMG_DEV, H, W, C)
    device_cot = cotangent.reshape(N_OUTER, N_INNER, IMG_DEV, H, W, E)

    def outer_fn(pair):
        inputs_outer, cot_outer = pair
        conv_sum = jnp.zeros((9 * C * C,), jnp.float32)
        expand_sum = jnp.zeros((C * E,), jnp.float32)
        grads_list = []
        for inner_pos in range(N_INNER):
            input_grad, conv_grad, expand_grad = local_step(inputs_outer[inner_pos], cot_outer[inner_pos], conv_weight, expand_weight)
            conv_sum = conv_sum + conv_grad.T.reshape(-1).astype(jnp.float32)
            expand_sum = expand_sum + expand_grad.reshape(-1).astype(jnp.float32)
            grads_list.append(input_grad)
        return jnp.stack(grads_list), conv_sum, expand_sum

    all_grads, conv_stack, expand_stack = lax.map(outer_fn, (device_inputs, device_cot))
    conv_final = adasum_levels(conv_stack)
    expand_final = adasum_levels(expand_stack)
    conv_new = MOMENTUM * conv_momentum + conv_final.reshape(DEVICES, S2)
    expand_new = MOMENTUM * expand_momentum + expand_final.reshape(DEVICES, S3)
    return all_grads.reshape(BATCH, H, W, C), conv_new, expand_new
```

```python
import jax
import jax.numpy as jnp
from jax import lax
from jax.experimental import pallas as pl
from jax.experimental.pallas import tpu as pltpu
from jax.sharding import PartitionSpec as P

EPS = 1e-06
MOMENTUM = 0.9
F32 = jnp.float32
BF16 = jnp.bfloat16
MESH = pl.DeviceIdType.MESH

PAIRS = 13
LAG2, LAG3, LAG4, LAG5, LAG6 = 1, 3, 4, 5, 7
GRAM = [(a, b) for a in range(8) for b in range(a, 8)]
GRAM_AT = {ab: n for n, ab in enumerate(GRAM)}


def nn(a, b):
    return lax.dot_general(a, b, (((1,), (0,)), ((), ())), preferred_element_type=F32)


def nt(a, b):
    return lax.dot_general(a, b, (((1,), (1,)), ((), ())), preferred_element_type=F32)


def adasum_weights(gram):
    count = 8
    weights = [None] * 8
    span = 1
    while count > 1:
        coefs = []
        for m in range(count // 2):
            a, b = 2 * m, 2 * m + 1
            dot = gram[(a, b)]
            coefs.append(
                (
                    1.0 - dot / (2.0 * (gram[(a, a)] + EPS)),
                    1.0 - dot / (2.0 * (gram[(b, b)] + EPS)),
                )
            )
        merged = {}
        for m in range(count // 2):
            for n in range(m, count // 2):
                total = None
                for s in range(2):
                    for t in range(2):
                        key = (min(2 * m + s, 2 * n + t), max(2 * m + s, 2 * n + t))
                        term = coefs[m][s] * coefs[n][t] * gram[key]
                        total = term if total is None else total + term
                merged[(m, n)] = jnp.maximum(total, 0.0) if m == n else total
        for o in range(8):
            group = o // span
            c = coefs[group // 2][group % 2]
            weights[o] = c if weights[o] is None else weights[o] * c
        gram = merged
        count //= 2
        span *= 2
    return weights


def kernel(
    x_hbm, cot_hbm, w_hbm, we_hbm,
    ig_hbm, fin_conv, fin_exp,
    xin, xs, wt, we, cot, acc, hp, ht, hg, hs, acc2, perm,
    gm, r1p, r1m, r2p, r2m, tb, r3p, r3m, r4p, r4m, ub, rx, gacc, stat, st1, st2,
    in_sem, w_sem, we_sem, cot_sem, out_sem,
    q1p, q1m, q2p, q2m, q3p, q3m, q4p, q4m, qx, qs1, qs2,
    s1p, s1m, s2p, s2m, s3p, s3m, s4p, s4m, sx, ss1, ss2,
):
    o = lax.axis_index("outer")
    i = lax.axis_index("inner")
    z = i // 4
    y = i % 4

    barrier = pltpu.get_barrier_semaphore()

    def greet_outer(d, carry):
        pl.semaphore_signal(barrier, inc=1, device_id={"outer": (o + d) % 8}, device_id_type=MESH)
        return carry

    def greet_inner(d, carry):
        pl.semaphore_signal(barrier, inc=1, device_id={"inner": (i + d) % 16}, device_id_type=MESH)
        return carry

    lax.fori_loop(1, 8, greet_outer, 0)
    lax.fori_loop(1, 16, greet_inner, 0)

    def w_copy(h, t):
        return pltpu.make_async_copy(
            w_hbm.at[pl.ds(pl.multiple_of(t * 512, 512), 512), pl.ds(pl.multiple_of(h * 256, 256), 256)],
            wt.at[h, t],
            w_sem.at[h, t],
        )

    def cot_copy(j):
        return pltpu.make_async_copy(cot_hbm.at[:, pl.ds(j * 512, 512)], cot.at[j], cot_sem.at[j])

    def we_copy(j):
        return pltpu.make_async_copy(we_hbm.at[:, pl.ds(j * 512, 512)], we.at[j], we_sem.at[j])

    in_copy = pltpu.make_async_copy(x_hbm, xin, in_sem)
    in_copy.start()

    def start_w(h):
        def one(t, carry):
            w_copy(h, t).start()
            return carry

        lax.fori_loop(0, 9, one, 0)

    start_w(0)
    for j in range(4):
        cot_copy(j).start()
    for j in range(4):
        we_copy(j).start()
    start_w(1)

    row = lax.broadcasted_iota(jnp.int32, (256, 256), 0)
    col = lax.broadcasted_iota(jnp.int32, (256, 256), 1)
    want = ((row // 4) % 4) * 64 + (row // 16) * 4 + row % 4
    perm[...] = jnp.where(want == col, 1.0, 0.0).astype(BF16)

    zero_row = jnp.zeros((16, 512), BF16)
    for dst in (xs, hs):
        for dx in range(3):
            for b in range(4):
                dst[dx, b, 0] = zero_row
                dst[dx, b, 17] = zero_row
    gacc[...] = jnp.zeros_like(gacc)

    def spread(value, dst, b, r, lanes):
        n = value.shape[1]
        w = lax.broadcasted_iota(jnp.int32, (64, n), 0) % 16
        wide = value.astype(F32)
        left = jnp.where(w == 0, 0.0, pltpu.roll(wide, 1, 0)).astype(BF16)
        right = jnp.where(w == 15, 0.0, pltpu.roll(wide, 63, 0)).astype(BF16)
        for dx, v in ((0, left), (1, value), (2, right)):
            dst[dx, b, pl.ds(1 + 4 * r, 4), :, lanes] = v.reshape(4, 16, n)

    in_copy.wait()

    def prep(g, carry):
        b, r = g // 4, g % 4
        v = xin[b, pl.ds(4 * r, 4)].reshape(64, 512)
        spread(jnp.maximum(v, jnp.zeros((), BF16)), xs, b, r, slice(None))
        return carry

    lax.fori_loop(0, 16, prep, 0)

    def tap(ref, t):
        return ref[t % 3, :, pl.ds(t // 3, 16)].reshape(1024, 512)

    def conv_taps(h, first, last):
        def one(t, carry):
            w_copy(h, t).wait()
            part = nn(tap(xs, t), wt[h, t])

            @pl.when(t == 0)
            def _():
                acc[...] = part

            @pl.when(t > 0)
            def _():
                acc[...] += part

            return carry

        lax.fori_loop(first, last, one, 0)

    def finish_forward(h):
        pre = acc[...].astype(BF16)
        hp[h] = pre
        ht[0, h] = nt(perm[...], jnp.maximum(pre, jnp.zeros((), BF16))).astype(BF16)

    def hidden_back(h, first, last):
        def one(k, carry):
            rows = pl.ds(pl.multiple_of(k * 256, 256), 256)
            chans = pl.ds(pl.multiple_of(h * 256, 256), 256)
            back = nt(cot[0, rows], we[0, chans])
            for j in range(1, 4):
                back = back + nt(cot[j, rows], we[j, chans])
            hg[h, rows] = jnp.where(hp[h, rows].astype(F32) > 0, back, 0.0).astype(BF16)
            return carry

        lax.fori_loop(first, last, one, 0)

    def finish_back(h):
        ht[1, h] = nt(perm[...], hg[h]).astype(BF16)

    def produce(p, k):
        q = 2 * p + k
        h = q // 13
        j = q % 13

        @pl.when(j < 4)
        def _():
            g = nn(ht[0, h], cot[j]) * (1.0 / 1024.0)
            gm[q] = g.astype(BF16).reshape(4, 4, 16, 512)

        @pl.when(j >= 4)
        def _():
            g = nn(ht[1, h], tap(xs, j - 4)) * (1.0 / 1024.0)
            gm[q] = g.astype(BF16).reshape(4, 4, 16, 512)

    def ring(k, stage):
        if (k + stage) % 2 == 0:
            return z, ((z + 1) % 4) * 4 + y, ((z + 3) % 4) * 4 + y
        return y, z * 4 + (y + 1) % 4, z * 4 + (y + 3) % 4

    def block(p, k, at):
        q = 2 * p + k
        return gm.at[q, at] if k == 0 else gm.at[q, :, at]

    def remote(src, dst, send, recv, inner):
        return pltpu.make_async_remote_copy(
            src_ref=src, dst_ref=dst, send_sem=send, recv_sem=recv,
            device_id={"inner": inner}, device_id_type=MESH,
        )

    LO, HI = slice(0, 256), slice(256, 512)

    def copies1(p, k):
        at, nxt, prv = ring(k, 0)
        far = block(p, k, (at + 2) % 4)
        return (
            remote(far.at[:, :, LO], r1p.at[p, k], s1p, q1p.at[p, k], nxt),
            remote(far.at[:, :, HI], r1m.at[p, k], s1m, q1m.at[p, k], prv),
        )

    def copies2(p, k):
        at, nxt, prv = ring(k, 0)
        return (
            remote(block(p, k, (at + 1) % 4), r2p.at[p, k], s2p, q2p.at[p, k], nxt),
            remote(block(p, k, (at + 3) % 4), r2m.at[p, k], s2m, q2m.at[p, k], prv),
        )

    def copies3(p, k):
        at, nxt, prv = ring(k, 1)
        far = tb.at[p, k, (at + 2) % 4]
        return (
            remote(far.at[:, LO], r3p.at[p, k], s3p, q3p.at[p, k], nxt),
            remote(far.at[:, HI], r3m.at[p, k], s3m, q3m.at[p, k], prv),
        )

    def copies4(p, k):
        at, nxt, prv = ring(k, 1)
        return (
            remote(tb.at[p, k, (at + 1) % 4], r4p.at[p, k], s4p, q4p.at[p, k], nxt),
            remote(tb.at[p, k, (at + 3) % 4], r4m.at[p, k], s4m, q4m.at[p, k], prv),
        )

    def step1(p, k):
        for c in copies1(p, k):
            c.start()

    def step2(p, k):
        at, _, _ = ring(k, 0)
        fwd, bwd = copies1(p, k)
        out_fwd, out_bwd = copies2(p, k)
        near = block(p, k, (at + 1) % 4)
        fwd.wait_recv()
        near[:, :, LO] = (near[:, :, LO].astype(F32) + r1p[p, k].astype(F32)).astype(BF16)
        out_fwd.start()
        near = block(p, k, (at + 3) % 4)
        bwd.wait_recv()
        near[:, :, HI] = (near[:, :, HI].astype(F32) + r1m[p, k].astype(F32)).astype(BF16)
        out_bwd.start()

    def step3(p, k):
        at, _, _ = ring(k, 0)
        for c in copies2(p, k):
            c.wait_recv()
        mine = block(p, k, at)
        total = mine[...].astype(F32) + r2p[p, k].astype(F32) + r2m[p, k].astype(F32)
        tb[p, k] = total.astype(BF16)
        for c in copies3(p, k):
            c.start()

    def step4(p, k):
        at, _, _ = ring(k, 1)
        fwd, bwd = copies3(p, k)
        out_fwd, out_bwd = copies4(p, k)
        near = tb.at[p, k, (at + 1) % 4]
        fwd.wait_recv()
        near[:, LO] = (near[:, LO].astype(F32) + r3p[p, k].astype(F32)).astype(BF16)
        out_fwd.start()
        near = tb.at[p, k, (at + 3) % 4]
        bwd.wait_recv()
        near[:, HI] = (near[:, HI].astype(F32) + r3m[p, k].astype(F32)).astype(BF16)
        out_bwd.start()

    def x_copy(p, k, part, j, dest):
        return pltpu.make_async_remote_copy(
            src_ref=ub.at[p, k, part], dst_ref=rx.at[j, o], send_sem=sx, recv_sem=qx.at[j],
            device_id={"outer": dest}, device_id_type=MESH,
        )

    def step5(p, k):
        at, _, _ = ring(k, 1)
        q = 2 * p + k
        h = q // 13
        j = q % 13
        for c in copies4(p, k):
            c.wait_recv()
        total = tb[p, k, at].astype(F32) + r4p[p, k].astype(F32) + r4m[p, k].astype(F32)
        for part in range(4):
            dest = h * 4 + part
            ub[p, k, part] = total[4 * part : 4 * part + 4]

            @pl.when(dest != o)
            def _():
                x_copy(p, k, part, j, dest).start()

            @pl.when(dest == o)
            def _():
                rx[j, o] = total[4 * part : 4 * part + 4]

    def step6(p, k):
        q = 2 * p + k
        j = q % 13

        @pl.when(q // 13 == o // 4)
        def _():
            pltpu.make_async_remote_copy(
                src_ref=rx.at[j, pl.ds(0, 7)], dst_ref=rx.at[j, pl.ds(0, 7)], send_sem=sx, recv_sem=qx.at[j],
                device_id={"outer": (o + 1) % 8}, device_id_type=MESH,
            ).wait_recv()
            kind = jnp.where(j < 4, 1, 0)
            vecs = [rx[j, a] for a in range(8)]
            for n, (a, b) in enumerate(GRAM):
                prod = vecs[a] * vecs[b]
                part = (prod[:, 0:128] + prod[:, 128:256]) + (prod[:, 256:384] + prod[:, 384:512])
                gacc[kind, n] = gacc[kind, n] + part

    conv_taps(0, 0, 9)
    finish_forward(0)
    for j in range(4):
        cot_copy(j).wait()
    for j in range(4):
        we_copy(j).wait()
    pl.semaphore_wait(barrier, 22)

    def image_rows(g, carry):
        b, r = g // 4, g % 4
        rows = pl.ds(pl.multiple_of(g * 64, 64), 64)
        for h in range(2):
            spread(hg[h, rows], hs, b, r, slice(h * 256, h * 256 + 256))
        return carry

    def input_taps(first, last):
        def one(t, carry):
            wide = tap(hs, t)
            part = nt(wide[:, 0:256], wt[0, 8 - t]) + nt(wide[:, 256:512], wt[1, 8 - t])

            @pl.when(t == 0)
            def _():
                acc2[...] = part

            @pl.when(t > 0)
            def _():
                acc2[...] += part

            return carry

        lax.fori_loop(first, last, one, 0)

    def finish_input():
        kept = jnp.where(xin[...].reshape(1024, 512).astype(F32) > 0, acc2[...], 0.0)
        xin[...] = kept.astype(BF16).reshape(4, 16, 16, 512)
        pltpu.make_async_copy(xin, ig_hbm, out_sem).start()

    def iteration(p, carry):
        for k in range(2):

            @pl.when(p < PAIRS)
            def _():
                produce(p, k)
                step1(p, k)

        for lag, step in ((LAG2, step2), (LAG3, step3), (LAG4, step4), (LAG5, step5), (LAG6, step6)):

            @pl.when(jnp.logical_and(p >= lag, p < PAIRS + lag))
            def _():
                for k in range(2):
                    step(p - lag, k)

        @pl.when(jnp.logical_or(p < 2, jnp.logical_or(p == 6, p == 7)))
        def _():
            h = p // 6
            k0 = (p % 2) * 2
            hidden_back(h, k0, k0 + 2)

            @pl.when(p % 2 == 1)
            def _():
                finish_back(h)

        @pl.when(jnp.logical_and(p >= 2, p < 6))
        def _():
            conv_taps(1, ((p - 2) * 9) // 4, ((p - 1) * 9) // 4)

            @pl.when(p == 5)
            def _():
                finish_forward(1)

        @pl.when(p == 8)
        def _():
            lax.fori_loop(0, 16, image_rows, 0)

        @pl.when(jnp.logical_and(p >= 8, p < 13))
        def _():
            input_taps(((p - 8) * 9) // 5, ((p - 7) * 9) // 5)

            @pl.when(p == 12)
            def _():
                finish_input()

        return carry

    lax.fori_loop(0, PAIRS + LAG6, iteration, 0)

    lane = lax.broadcasted_iota(jnp.int32, (1, 128), 1)
    rows = []
    for kind in range(2):
        packed = jnp.zeros((1, 128), F32)
        for n in range(len(GRAM)):
            line = jnp.sum(gacc[kind, n], axis=0, keepdims=True)
            packed = jnp.where(lane == n, jnp.sum(line, axis=1, keepdims=True), packed)
        rows.append(packed)
    sub = lax.broadcasted_iota(jnp.int32, (8, 128), 0)
    mine = jnp.where(sub == 0, rows[0], jnp.where(sub == 1, rows[1], 0.0))

    def exchange(axis, me, count, value, src, dst, send, recv):
        src[...] = value
        dst[me] = value

        def go(d, carry):
            pltpu.make_async_remote_copy(
                src_ref=src, dst_ref=dst.at[me], send_sem=send, recv_sem=recv,
                device_id={axis: (me + d) % count}, device_id_type=MESH,
            ).start()
            return carry

        lax.fori_loop(1, count, go, 0)
        got = dst.at[pl.ds(0, count - 1)]
        pltpu.make_async_remote_copy(
            src_ref=got, dst_ref=got, send_sem=send, recv_sem=recv,
            device_id={axis: (me + 1) % count}, device_id_type=MESH,
        ).wait_recv()
        total = dst[0]
        for n in range(1, count):
            total = total + dst[n]
        return total

    total = exchange("outer", o, 8, mine, stat.at[0], st1, ss1, qs1)
    total = exchange("inner", i, 16, total, stat.at[1], st2, ss2, qs2)
    gram = {ab: jnp.broadcast_to(total[:, n : n + 1], (8, 128)) for ab, n in GRAM_AT.items()}
    weights = adasum_weights(gram)

    for kind, count, out in ((0, 9, fin_conv), (1, 4, fin_exp)):
        coef = [jnp.broadcast_to(jnp.tile(w[kind : kind + 1], (1, 4)), (4, 512)) for w in weights]
        for t in range(count):
            j = t if kind == 1 else t + 4
            value = coef[0] * rx[j, 0]
            for a in range(1, 8):
                value = value + coef[a] * rx[j, a]
            out[:, t * 512 : (t + 1) * 512] = value

    def drain(ref, send):
        pltpu.make_async_remote_copy(
            src_ref=ref, dst_ref=ref, send_sem=send, recv_sem=qs1,
            device_id={"outer": (o + 1) % 8}, device_id_type=MESH,
        ).wait_send()

    for ref, send in (
        (r1p, s1p), (r1m, s1m), (r2p, s2p), (r2m, s2m), (r3p, s3p), (r3m, s3m), (r4p, s4p), (r4m, s4m),
        (rx.at[:, pl.ds(0, 7)], sx), (st1.at[pl.ds(0, 7)], ss1), (st2.at[pl.ds(0, 15)], ss2),
    ):
        drain(ref, send)
    pltpu.make_async_copy(xin, ig_hbm, out_sem).wait()


def body(inputs, cotangent, conv_weight, expand_weight, conv_momentum, expand_momentum):
    images, height, across, channels = inputs.shape
    rows = images * height * across
    dma = pltpu.SemaphoreType.DMA
    vmem = pltpu.VMEM
    any_spec = pl.BlockSpec(memory_space=pl.ANY)
    vmem_spec = pl.BlockSpec(memory_space=pltpu.VMEM)
    input_grad, fin_conv, fin_exp = pl.pallas_call(
        kernel,
        out_shape=(
            jax.ShapeDtypeStruct(inputs.shape, BF16),
            jax.ShapeDtypeStruct((4, 4608), F32),
            jax.ShapeDtypeStruct((4, 2048), F32),
        ),
        in_specs=[any_spec] * 4,
        out_specs=(any_spec, vmem_spec, vmem_spec),
        scratch_shapes=[
            vmem((4, 16, 16, 512), BF16),
            vmem((3, 4, 18, 16, 512), BF16),
            vmem((2, 9, 512, 256), BF16),
            vmem((4, 512, 512), BF16),
            vmem((4, 1024, 512), BF16),
            vmem((1024, 256), F32),
            vmem((2, 1024, 256), BF16),
            vmem((2, 2, 256, 1024), BF16),
            vmem((2, 1024, 256), BF16),
            vmem((3, 4, 18, 16, 512), BF16),
            vmem((1024, 512), F32),
            vmem((256, 256), BF16),
            vmem((26, 4, 4, 16, 512), BF16),
            vmem((PAIRS, 2, 4, 16, 256), BF16),
            vmem((PAIRS, 2, 4, 16, 256), BF16),
            vmem((PAIRS, 2, 4, 16, 512), BF16),
            vmem((PAIRS, 2, 4, 16, 512), BF16),
            vmem((PAIRS, 2, 4, 16, 512), BF16),
            vmem((PAIRS, 2, 16, 256), BF16),
            vmem((PAIRS, 2, 16, 256), BF16),
            vmem((PAIRS, 2, 16, 512), BF16),
            vmem((PAIRS, 2, 16, 512), BF16),
            vmem((PAIRS, 2, 4, 4, 512), F32),
            vmem((13, 8, 4, 512), F32),
            vmem((2, len(GRAM), 4, 128), F32),
            vmem((2, 8, 128), F32),
            vmem((8, 8, 128), F32),
            vmem((16, 8, 128), F32),
            dma, dma((2, 9)), dma((4,)), dma((4,)), dma,
        ]
        + [dma((PAIRS, 2))] * 8
        + [dma((13,)), dma, dma]
        + [dma] * 11,
        compiler_params=pltpu.CompilerParams(
            collective_id=0, has_side_effects=True, vmem_limit_bytes=62 * 1024 * 1024
        ),
    )(inputs, cotangent.reshape(rows, cotangent.shape[-1]), conv_weight, expand_weight)
    conv_new = MOMENTUM * conv_momentum + fin_conv.reshape(conv_momentum.shape)
    expand_new = MOMENTUM * expand_momentum + fin_exp.reshape(expand_momentum.shape)
    return (input_grad, conv_new, expand_new)


def solution(mesh):
    return jax.shard_map(
        body,
        mesh=mesh,
        in_specs=(
            P(("outer", "inner"), None, None, None),
            P(("outer", "inner"), None, None, None),
            P(),
            P(),
            P(("outer", "inner"), None),
            P(("outer", "inner"), None),
        ),
        out_specs=(
            P(("outer", "inner"), None, None, None),
            P(("outer", "inner"), None),
            P(("outer", "inner"), None),
        ),
        check_vma=False,
    )
```

```python
import jax
import jax.numpy as jnp
from jax import lax
from jax.experimental import pallas as pl
from jax.experimental.pallas import tpu as pltpu
from jax.sharding import PartitionSpec as P

EPS = 1e-06
MOMENTUM = 0.9
F32 = jnp.float32
BF16 = jnp.bfloat16
MESH = pl.DeviceIdType.MESH

PAIRS = 13
LAG2, LAG3, LAG4, LAG5, LAG6 = 2, 4, 6, 8, 10
INPUT_AT = 9
GRAM = [(a, b) for a in range(8) for b in range(a, 8)]
GRAM_AT = {ab: n for n, ab in enumerate(GRAM)}


def nn(a, b):
    return lax.dot_general(a, b, (((1,), (0,)), ((), ())), preferred_element_type=F32)


def nt(a, b):
    return lax.dot_general(a, b, (((1,), (1,)), ((), ())), preferred_element_type=F32)


def adasum_weights(gram):
    count = 8
    weights = [None] * 8
    span = 1
    while count > 1:
        coefs = []
        for m in range(count // 2):
            a, b = 2 * m, 2 * m + 1
            dot = gram[(a, b)]
            coefs.append(
                (
                    1.0 - dot / (2.0 * (gram[(a, a)] + EPS)),
                    1.0 - dot / (2.0 * (gram[(b, b)] + EPS)),
                )
            )
        merged = {}
        for m in range(count // 2):
            for n in range(m, count // 2):
                total = None
                for s in range(2):
                    for t in range(2):
                        key = (min(2 * m + s, 2 * n + t), max(2 * m + s, 2 * n + t))
                        term = coefs[m][s] * coefs[n][t] * gram[key]
                        total = term if total is None else total + term
                merged[(m, n)] = jnp.maximum(total, 0.0) if m == n else total
        for o in range(8):
            group = o // span
            c = coefs[group // 2][group % 2]
            weights[o] = c if weights[o] is None else weights[o] * c
        gram = merged
        count //= 2
        span *= 2
    return weights


def kernel(
    x_hbm, cot_hbm, w_hbm, we_hbm,
    ig_hbm, fin_conv, fin_exp,
    xin, xs, wt, wn, we, cot, acc, hp, ht, hg, hs, acc2, perm,
    gm, r1p, r1m, r2p, r2m, tb, r3p, r3m, r4p, r4m, ub, rx, gacc, stat, st1, st2,
    in_sem, w_sem, wn_sem, we_sem, cot_sem, out_sem,
    q1p, q1m, q2p, q2m, q3p, q3m, q4p, q4m, qx, qs1, qs2,
    s1p, s1m, s2p, s2m, s3p, s3m, s4p, s4m, sx, ss1, ss2,
):
    o = lax.axis_index("outer")
    i = lax.axis_index("inner")
    z = i // 4
    y = i % 4

    barrier = pltpu.get_barrier_semaphore()

    def greet_outer(d, carry):
        pl.semaphore_signal(barrier, inc=1, device_id={"outer": (o + d) % 8}, device_id_type=MESH)
        return carry

    def greet_inner(d, carry):
        pl.semaphore_signal(barrier, inc=1, device_id={"inner": (i + d) % 16}, device_id_type=MESH)
        return carry

    lax.fori_loop(1, 8, greet_outer, 0)
    lax.fori_loop(1, 16, greet_inner, 0)

    def w_copy(h, dy):
        return pltpu.make_async_copy(
            w_hbm.at[pl.ds(dy * 1536, 1536), pl.ds(h * 256, 256)], wt.at[h, dy], w_sem.at[h, dy]
        )

    def wn_copies(ty):
        return [
            pltpu.make_async_copy(
                w_hbm.at[pl.ds(((2 - ty) * 3 + 2 - tx) * 512, 512)],
                wn.at[ty, :, pl.ds(tx * 512, 512)],
                wn_sem.at[ty, tx],
            )
            for tx in range(3)
        ]

    cot_copy = pltpu.make_async_copy(cot_hbm, cot, cot_sem)
    we_copy = pltpu.make_async_copy(we_hbm, we, we_sem)
    in_copy = pltpu.make_async_copy(x_hbm, xin, in_sem)
    in_copy.start()
    for dy in range(3):
        w_copy(0, dy).start()
    cot_copy.start()
    we_copy.start()
    for dy in range(3):
        w_copy(1, dy).start()
    for ty in range(3):
        for c in wn_copies(ty):
            c.start()

    row = lax.broadcasted_iota(jnp.int32, (256, 256), 0)
    col = lax.broadcasted_iota(jnp.int32, (256, 256), 1)
    want = ((row // 4) % 4) * 64 + (row // 16) * 4 + row % 4
    perm[...] = jnp.where(want == col, 1.0, 0.0).astype(BF16)

    zero_row = jnp.zeros((16, 1536), BF16)
    for dst in (xs, hs):
        for b in range(4):
            dst[b, 0] = zero_row
            dst[b, 17] = zero_row
    gacc[...] = jnp.zeros_like(gacc)

    def spread(value, dst, b, r, first):
        n = value.shape[1]
        w = lax.broadcasted_iota(jnp.int32, (64, n), 0) % 16
        wide = value.astype(F32)
        left = jnp.where(w == 0, 0.0, pltpu.roll(wide, 1, 0)).astype(BF16)
        right = jnp.where(w == 15, 0.0, pltpu.roll(wide, 63, 0)).astype(BF16)
        for dx, v in ((0, left), (1, value), (2, right)):
            at = dx * 512 + first
            dst[b, pl.ds(1 + 4 * r, 4), :, at : at + n] = v.reshape(4, 16, n)

    in_copy.wait()

    def prep(g, carry):
        b, r = g // 4, g % 4
        v = xin[b, pl.ds(4 * r, 4)].reshape(64, 512)
        spread(jnp.maximum(v, jnp.zeros((), BF16)), xs, b, r, 0)
        return carry

    lax.fori_loop(0, 16, prep, 0)

    def tap_row(ref, dy):
        return ref[:, pl.ds(dy, 16)].reshape(1024, 1536)

    def conv_taps(h, dy, first):
        w_copy(h, dy).wait()
        part = nn(tap_row(xs, dy), wt[h, dy])
        if first:
            acc[...] = part
        else:
            acc[...] += part

    def finish_forward(h):
        pre = acc[...].astype(BF16)
        hp[h] = pre
        ht[0, h] = nt(perm[...], jnp.maximum(pre, jnp.zeros((), BF16))).astype(BF16)

    def hidden_back(h, k):
        rows = pl.ds(pl.multiple_of(k * 512, 512), 512)
        chans = pl.ds(pl.multiple_of(h * 256, 256), 256)
        back = nt(cot[rows], we[chans])
        hg[h, rows] = jnp.where(hp[h, rows].astype(F32) > 0, back, 0.0).astype(BF16)

    def finish_back(h):
        ht[1, h] = nt(perm[...], hg[h]).astype(BF16)

    def produce(p, k):
        q = 2 * p + k
        h = q // 13
        j = q % 13

        @pl.when(j < 4)
        def _():
            g = nn(ht[0, h], cot[:, pl.ds(pl.multiple_of(j * 512, 512), 512)]) * (1.0 / 1024.0)
            gm[q] = g.astype(BF16).reshape(4, 4, 16, 512)

        @pl.when(j >= 4)
        def _():
            t = j - 4
            at = pl.multiple_of((t % 3) * 512, 512)
            g = nn(ht[1, h], xs[:, pl.ds(t // 3, 16), :, pl.ds(at, 512)].reshape(1024, 512)) * (1.0 / 1024.0)
            gm[q] = g.astype(BF16).reshape(4, 4, 16, 512)

    def ring(k, stage):
        if (k + stage) % 2 == 0:
            return z, ((z + 1) % 4) * 4 + y, ((z + 3) % 4) * 4 + y
        return y, z * 4 + (y + 1) % 4, z * 4 + (y + 3) % 4

    def block(p, k, at):
        q = 2 * p + k
        return gm.at[q, at] if k == 0 else gm.at[q, :, at]

    def remote(src, dst, send, recv, inner):
        return pltpu.make_async_remote_copy(
            src_ref=src, dst_ref=dst, send_sem=send, recv_sem=recv,
            device_id={"inner": inner}, device_id_type=MESH,
        )

    LO, HI = slice(0, 256), slice(256, 512)

    def copies1(p, k):
        at, nxt, prv = ring(k, 0)
        far = block(p, k, (at + 2) % 4)
        return (
            remote(far.at[:, :, LO], r1p.at[p, k], s1p, q1p.at[p, k], nxt),
            remote(far.at[:, :, HI], r1m.at[p, k], s1m, q1m.at[p, k], prv),
        )

    def copies2(p, k):
        at, nxt, prv = ring(k, 0)
        return (
            remote(block(p, k, (at + 1) % 4), r2p.at[p, k], s2p, q2p.at[p, k], nxt),
            remote(block(p, k, (at + 3) % 4), r2m.at[p, k], s2m, q2m.at[p, k], prv),
        )

    def copies3(p, k):
        at, nxt, prv = ring(k, 1)
        far = tb.at[p, k, (at + 2) % 4]
        return (
            remote(far.at[:, LO], r3p.at[p, k], s3p, q3p.at[p, k], nxt),
            remote(far.at[:, HI], r3m.at[p, k], s3m, q3m.at[p, k], prv),
        )

    def copies4(p, k):
        at, nxt, prv = ring(k, 1)
        return (
            remote(tb.at[p, k, (at + 1) % 4], r4p.at[p, k], s4p, q4p.at[p, k], nxt),
            remote(tb.at[p, k, (at + 3) % 4], r4m.at[p, k], s4m, q4m.at[p, k], prv),
        )

    def step1(p, k):
        for c in copies1(p, k):
            c.start()

    def step2(p, k):
        at, _, _ = ring(k, 0)
        fwd, bwd = copies1(p, k)
        out_fwd, out_bwd = copies2(p, k)
        near = block(p, k, (at + 1) % 4)
        fwd.wait_recv()
        near[:, :, LO] = (near[:, :, LO].astype(F32) + r1p[p, k].astype(F32)).astype(BF16)
        out_fwd.start()
        near = block(p, k, (at + 3) % 4)
        bwd.wait_recv()
        near[:, :, HI] = (near[:, :, HI].astype(F32) + r1m[p, k].astype(F32)).astype(BF16)
        out_bwd.start()

    def step3(p, k):
        at, _, _ = ring(k, 0)
        for c in copies2(p, k):
            c.wait_recv()
        mine = block(p, k, at)
        total = mine[...].astype(F32) + r2p[p, k].astype(F32) + r2m[p, k].astype(F32)
        tb[p, k] = total.astype(BF16)
        for c in copies3(p, k):
            c.start()

    def step4(p, k):
        at, _, _ = ring(k, 1)
        fwd, bwd = copies3(p, k)
        out_fwd, out_bwd = copies4(p, k)
        near = tb.at[p, k, (at + 1) % 4]
        fwd.wait_recv()
        near[:, LO] = (near[:, LO].astype(F32) + r3p[p, k].astype(F32)).astype(BF16)
        out_fwd.start()
        near = tb.at[p, k, (at + 3) % 4]
        bwd.wait_recv()
        near[:, HI] = (near[:, HI].astype(F32) + r3m[p, k].astype(F32)).astype(BF16)
        out_bwd.start()

    def x_copy(p, k, part, j, dest):
        return pltpu.make_async_remote_copy(
            src_ref=ub.at[p, k, part], dst_ref=rx.at[j, o], send_sem=sx, recv_sem=qx.at[j],
            device_id={"outer": dest}, device_id_type=MESH,
        )

    def step5(p, k):
        at, _, _ = ring(k, 1)
        q = 2 * p + k
        h = q // 13
        j = q % 13
        for c in copies4(p, k):
            c.wait_recv()
        total = tb[p, k, at].astype(F32) + r4p[p, k].astype(F32) + r4m[p, k].astype(F32)
        for part in range(4):
            dest = h * 4 + part
            ub[p, k, part] = total[4 * part : 4 * part + 4]

            @pl.when(dest != o)
            def _():
                x_copy(p, k, part, j, dest).start()

            @pl.when(dest == o)
            def _():
                rx[j, o] = total[4 * part : 4 * part + 4]

    def step6(p, k):
        q = 2 * p + k
        j = q % 13

        @pl.when(q // 13 == o // 4)
        def _():
            pltpu.make_async_remote_copy(
                src_ref=rx.at[j, pl.ds(0, 7)], dst_ref=rx.at[j, pl.ds(0, 7)], send_sem=sx, recv_sem=qx.at[j],
                device_id={"outer": (o + 1) % 8}, device_id_type=MESH,
            ).wait_recv()
            kind = jnp.where(j < 4, 1, 0)
            vecs = [rx[j, a] for a in range(8)]
            for n, (a, b) in enumerate(GRAM):
                prod = vecs[a] * vecs[b]
                part = (prod[:, 0:128] + prod[:, 128:256]) + (prod[:, 256:384] + prod[:, 384:512])
                gacc[kind, n] = gacc[kind, n] + part

    for dy in range(3):
        conv_taps(0, dy, dy == 0)
    finish_forward(0)
    cot_copy.wait()
    we_copy.wait()
    pl.semaphore_wait(barrier, 22)

    def image_rows(g, carry):
        b, r = g // 4, g % 4
        rows = pl.ds(pl.multiple_of(g * 64, 64), 64)
        for h in range(2):
            spread(hg[h, rows], hs, b, r, h * 256)
        return carry

    def input_piece(ty, m):
        part = nt(hs[pl.ds(2 * m, 2), pl.ds(ty, 16)].reshape(512, 1536), wn[ty])
        rows = pl.ds(pl.multiple_of(512 * m, 512), 512)
        if ty == 0:
            acc2[rows] = part
        elif ty == 1:
            acc2[rows] += part
        else:
            images = pl.ds(2 * m, 2)
            total = acc2[rows] + part
            kept = jnp.where(xin[images].reshape(512, 512).astype(F32) > 0, total, 0.0)
            xin[images] = kept.astype(BF16).reshape(2, 16, 16, 512)

    def input_work(p):
        @pl.when(p == INPUT_AT - 1)
        def _():
            lax.fori_loop(0, 16, image_rows, 0)

        for ty in range(3):

            @pl.when(jnp.logical_and(p >= INPUT_AT + 2 * ty, p < INPUT_AT + 2 * ty + 2))
            def _():
                m = p - (INPUT_AT + 2 * ty)

                @pl.when(m == 0)
                def _():
                    for c in wn_copies(ty):
                        c.wait()

                input_piece(ty, m)

        @pl.when(p == INPUT_AT + 5)
        def _():
            pltpu.make_async_copy(xin, ig_hbm, out_sem).start()

    def iteration(p, carry):
        for k in range(2):

            @pl.when(p < PAIRS)
            def _():
                produce(p, k)
                step1(p, k)

        for lag, step in ((LAG2, step2), (LAG3, step3), (LAG4, step4), (LAG5, step5), (LAG6, step6)):

            @pl.when(jnp.logical_and(p >= lag, p < PAIRS + lag))
            def _():
                for k in range(2):
                    step(p - lag, k)

        @pl.when(jnp.logical_or(p < 2, jnp.logical_or(p == 6, p == 7)))
        def _():
            h = p // 6
            hidden_back(h, p % 2)

            @pl.when(p % 2 == 1)
            def _():
                finish_back(h)

        @pl.when(p == 2)
        def _():
            conv_taps(1, 0, True)

        @pl.when(jnp.logical_or(p == 3, p == 4))
        def _():
            conv_taps(1, p - 2, False)

            @pl.when(p == 4)
            def _():
                finish_forward(1)

        input_work(p)
        return carry

    lax.fori_loop(0, PAIRS + LAG6, iteration, 0)

    lane = lax.broadcasted_iota(jnp.int32, (1, 128), 1)
    rows = []
    for kind in range(2):
        packed = jnp.zeros((1, 128), F32)
        for n in range(len(GRAM)):
            line = jnp.sum(gacc[kind, n], axis=0, keepdims=True)
            packed = jnp.where(lane == n, jnp.sum(line, axis=1, keepdims=True), packed)
        rows.append(packed)
    sub = lax.broadcasted_iota(jnp.int32, (8, 128), 0)
    mine = jnp.where(sub == 0, rows[0], jnp.where(sub == 1, rows[1], 0.0))

    def exchange(axis, me, count, value, src, dst, send, recv):
        src[...] = value
        dst[me] = value

        def go(d, carry):
            pltpu.make_async_remote_copy(
                src_ref=src, dst_ref=dst.at[me], send_sem=send, recv_sem=recv,
                device_id={axis: (me + d) % count}, device_id_type=MESH,
            ).start()
            return carry

        lax.fori_loop(1, count, go, 0)
        got = dst.at[pl.ds(0, count - 1)]
        pltpu.make_async_remote_copy(
            src_ref=got, dst_ref=got, send_sem=send, recv_sem=recv,
            device_id={axis: (me + 1) % count}, device_id_type=MESH,
        ).wait_recv()
        total = dst[0]
        for n in range(1, count):
            total = total + dst[n]
        return total

    total = exchange("outer", o, 8, mine, stat.at[0], st1, ss1, qs1)
    total = exchange("inner", i, 16, total, stat.at[1], st2, ss2, qs2)
    gram = {ab: jnp.broadcast_to(total[:, n : n + 1], (8, 128)) for ab, n in GRAM_AT.items()}
    weights = adasum_weights(gram)

    for kind, count, out in ((0, 9, fin_conv), (1, 4, fin_exp)):
        coef = [jnp.broadcast_to(jnp.tile(w[kind : kind + 1], (1, 4)), (4, 512)) for w in weights]
        for t in range(count):
            j = t if kind == 1 else t + 4
            value = coef[0] * rx[j, 0]
            for a in range(1, 8):
                value = value + coef[a] * rx[j, a]
            out[:, t * 512 : (t + 1) * 512] = value

    def drain(ref, send):
        pltpu.make_async_remote_copy(
            src_ref=ref, dst_ref=ref, send_sem=send, recv_sem=qs1,
            device_id={"outer": (o + 1) % 8}, device_id_type=MESH,
        ).wait_send()

    for ref, send in (
        (r1p, s1p), (r1m, s1m), (r2p, s2p), (r2m, s2m), (r3p, s3p), (r3m, s3m), (r4p, s4p), (r4m, s4m),
        (rx.at[:, pl.ds(0, 7)], sx), (st1.at[pl.ds(0, 7)], ss1), (st2.at[pl.ds(0, 15)], ss2),
    ):
        drain(ref, send)
    pltpu.make_async_copy(xin, ig_hbm, out_sem).wait()


def update_kernel(ig, fin_conv, fin_exp, mom_conv, mom_exp, ig_out, new_conv, new_exp, buf, in_sem, out_sem):
    def fetch(b):
        return pltpu.make_async_copy(ig.at[b], buf.at[b], in_sem.at[b])

    def put(b):
        return pltpu.make_async_copy(buf.at[b], ig_out.at[b], out_sem.at[b])

    for b in range(4):
        fetch(b).start()
    for fin, mom, new in ((fin_conv, mom_conv, new_conv), (fin_exp, mom_exp, new_exp)):
        n = fin.shape[1]
        for s in range(4):
            new[0:1, s * n : (s + 1) * n] = MOMENTUM * mom[0:1, s * n : (s + 1) * n] + fin[s : s + 1, :]
    for b in range(4):
        fetch(b).wait()
        put(b).start()
    for b in range(4):
        put(b).wait()


def body(inputs, cotangent, conv_weight, expand_weight, conv_momentum, expand_momentum):
    images, height, across, channels = inputs.shape
    rows = images * height * across
    dma = pltpu.SemaphoreType.DMA
    vmem = pltpu.VMEM
    any_spec = pl.BlockSpec(memory_space=pl.ANY)
    vmem_spec = pl.BlockSpec(memory_space=pltpu.VMEM)
    input_grad, fin_conv, fin_exp = pl.pallas_call(
        kernel,
        out_shape=(
            jax.ShapeDtypeStruct(inputs.shape, BF16),
            jax.ShapeDtypeStruct((4, 4608), F32),
            jax.ShapeDtypeStruct((4, 2048), F32),
        ),
        in_specs=[any_spec] * 4,
        out_specs=(any_spec, vmem_spec, vmem_spec),
        scratch_shapes=[
            vmem((4, 16, 16, 512), BF16),
            vmem((4, 18, 16, 1536), BF16),
            vmem((2, 3, 1536, 256), BF16),
            vmem((3, 512, 1536), BF16),
            vmem((512, 2048), BF16),
            vmem((1024, 2048), BF16),
            vmem((1024, 256), F32),
            vmem((2, 1024, 256), BF16),
            vmem((2, 2, 256, 1024), BF16),
            vmem((2, 1024, 256), BF16),
            vmem((4, 18, 16, 1536), BF16),
            vmem((1024, 512), F32),
            vmem((256, 256), BF16),
            vmem((26, 4, 4, 16, 512), BF16),
            vmem((PAIRS, 2, 4, 16, 256), BF16),
            vmem((PAIRS, 2, 4, 16, 256), BF16),
            vmem((PAIRS, 2, 4, 16, 512), BF16),
            vmem((PAIRS, 2, 4, 16, 512), BF16),
            vmem((PAIRS, 2, 4, 16, 512), BF16),
            vmem((PAIRS, 2, 16, 256), BF16),
            vmem((PAIRS, 2, 16, 256), BF16),
            vmem((PAIRS, 2, 16, 512), BF16),
            vmem((PAIRS, 2, 16, 512), BF16),
            vmem((PAIRS, 2, 4, 4, 512), F32),
            vmem((13, 8, 4, 512), F32),
            vmem((2, len(GRAM), 4, 128), F32),
            vmem((2, 8, 128), F32),
            vmem((8, 8, 128), F32),
            vmem((16, 8, 128), F32),
            dma, dma((2, 3)), dma((3, 3)), dma, dma, dma,
        ]
        + [dma((PAIRS, 2))] * 8
        + [dma((13,)), dma, dma]
        + [dma] * 11,
        compiler_params=pltpu.CompilerParams(
            collective_id=0, has_side_effects=True, vmem_limit_bytes=62 * 1024 * 1024
        ),
    )(inputs, cotangent.reshape(rows, cotangent.shape[-1]), conv_weight, expand_weight)
    return pl.pallas_call(
        update_kernel,
        out_shape=(
            jax.ShapeDtypeStruct(inputs.shape, BF16),
            jax.ShapeDtypeStruct(conv_momentum.shape, F32),
            jax.ShapeDtypeStruct(expand_momentum.shape, F32),
        ),
        in_specs=[any_spec] + [vmem_spec] * 4,
        out_specs=(any_spec, vmem_spec, vmem_spec),
        scratch_shapes=[vmem((4, 16, 16, 512), BF16), dma((4,)), dma((4,))],
    )(input_grad, fin_conv, fin_exp, conv_momentum, expand_momentum)


def solution(mesh):
    return jax.shard_map(
        body,
        mesh=mesh,
        in_specs=(
            P(("outer", "inner"), None, None, None),
            P(("outer", "inner"), None, None, None),
            P(),
            P(),
            P(("outer", "inner"), None),
            P(("outer", "inner"), None),
        ),
        out_specs=(
            P(("outer", "inner"), None, None, None),
            P(("outer", "inner"), None),
            P(("outer", "inner"), None),
        ),
        check_vma=False,
    )
```

```python
import jax
import jax.numpy as jnp
from jax import lax
from jax.experimental import pallas as pl
from jax.experimental.pallas import tpu as pltpu
from jax.sharding import PartitionSpec as P

EPS = 1e-06
MOMENTUM = 0.9
F32 = jnp.float32
BF16 = jnp.bfloat16
MESH = pl.DeviceIdType.MESH

PAIRS = 13
LAG2, LAG3, LAG4, LAG5, LAG6 = 2, 4, 6, 8, 10
INPUT_AT = 9
VMEM_LIMIT = 56 * 1024 * 1024
GRAM = [(a, b) for a in range(8) for b in range(a, 8)]
GRAM_AT = {ab: n for n, ab in enumerate(GRAM)}


def nn(a, b):
    return lax.dot_general(a, b, (((1,), (0,)), ((), ())), preferred_element_type=F32)


def nt(a, b):
    return lax.dot_general(a, b, (((1,), (1,)), ((), ())), preferred_element_type=F32)


def adasum_weights(gram):
    count = 8
    weights = [None] * 8
    span = 1
    while count > 1:
        coefs = []
        for m in range(count // 2):
            a, b = 2 * m, 2 * m + 1
            dot = gram[(a, b)]
            coefs.append(
                (
                    1.0 - dot / (2.0 * (gram[(a, a)] + EPS)),
                    1.0 - dot / (2.0 * (gram[(b, b)] + EPS)),
                )
            )
        merged = {}
        for m in range(count // 2):
            for n in range(m, count // 2):
                total = None
                for s in range(2):
                    for t in range(2):
                        key = (min(2 * m + s, 2 * n + t), max(2 * m + s, 2 * n + t))
                        term = coefs[m][s] * coefs[n][t] * gram[key]
                        total = term if total is None else total + term
                merged[(m, n)] = jnp.maximum(total, 0.0) if m == n else total
        for o in range(8):
            group = o // span
            c = coefs[group // 2][group % 2]
            weights[o] = c if weights[o] is None else weights[o] * c
        gram = merged
        count //= 2
        span *= 2
    return weights


def kernel(
    x_hbm, cot_hbm, w_hbm, we_hbm,
    ig, fin_conv, fin_exp,
    xin, xs, wt, wn, we, cot, acc, hp, ht, hg, hs, acc2, perm,
    gm, r1p, r1m, r2p, r2m, tb, r3p, r3m, r4p, r4m, ub, rx, gacc, stat, st1, st2,
    in_sem, w_sem, wn_sem, we_sem, cot_sem,
    q1p, q1m, q2p, q2m, q3p, q3m, q4p, q4m, qx, qs1, qs2,
    s1p, s1m, s2p, s2m, s3p, s3m, s4p, s4m, sx, ss1, ss2,
):
    o = lax.axis_index("outer")
    i = lax.axis_index("inner")
    z = i // 4
    y = i % 4

    barrier = pltpu.get_barrier_semaphore()

    def greet_outer(d, carry):
        pl.semaphore_signal(barrier, inc=1, device_id={"outer": (o + d) % 8}, device_id_type=MESH)
        return carry

    def greet_inner(d, carry):
        pl.semaphore_signal(barrier, inc=1, device_id={"inner": (i + d) % 16}, device_id_type=MESH)
        return carry

    lax.fori_loop(1, 8, greet_outer, 0)
    lax.fori_loop(1, 16, greet_inner, 0)

    def w_copy(h, dy):
        return pltpu.make_async_copy(
            w_hbm.at[pl.ds(dy * 1536, 1536), pl.ds(h * 256, 256)], wt.at[h, dy], w_sem.at[h, dy]
        )

    def wn_copies(ty):
        return [
            pltpu.make_async_copy(
                w_hbm.at[pl.ds(((2 - ty) * 3 + 2 - tx) * 512, 512)],
                wn.at[ty, :, pl.ds(tx * 512, 512)],
                wn_sem.at[ty, tx],
            )
            for tx in range(3)
        ]

    cot_copy = pltpu.make_async_copy(cot_hbm, cot, cot_sem)
    we_copy = pltpu.make_async_copy(we_hbm, we, we_sem)
    in_copies = [pltpu.make_async_copy(x_hbm.at[b], xin.at[b], in_sem.at[b]) for b in range(4)]
    for c in in_copies:
        c.start()
    for dy in range(3):
        w_copy(0, dy).start()
    cot_copy.start()
    we_copy.start()
    for dy in range(3):
        w_copy(1, dy).start()
    for ty in range(3):
        for c in wn_copies(ty):
            c.start()

    row = lax.broadcasted_iota(jnp.int32, (256, 256), 0)
    col = lax.broadcasted_iota(jnp.int32, (256, 256), 1)
    want = ((row // 4) % 4) * 64 + (row // 16) * 4 + row % 4
    perm[...] = jnp.where(want == col, 1.0, 0.0).astype(BF16)

    zero_row = jnp.zeros((16, 1536), BF16)
    for dst in (xs, hs):
        for b in range(4):
            dst[b, 0] = zero_row
            dst[b, 17] = zero_row
    gacc[...] = jnp.zeros_like(gacc)

    def spread(value, dst, b, r, first):
        n = value.shape[1]
        w = lax.broadcasted_iota(jnp.int32, (64, n), 0) % 16
        wide = value.astype(F32)
        left = jnp.where(w == 0, 0.0, pltpu.roll(wide, 1, 0)).astype(BF16)
        right = jnp.where(w == 15, 0.0, pltpu.roll(wide, 63, 0)).astype(BF16)
        for dx, v in ((0, left), (1, value), (2, right)):
            at = dx * 512 + first
            dst[b, pl.ds(1 + 4 * r, 4), :, at : at + n] = v.reshape(4, 16, n)


    for b in range(4):
        in_copies[b].wait()

        def prep(r, carry, b=b):
            v = xin[b, pl.ds(4 * r, 4)].reshape(64, 512)
            spread(jnp.maximum(v, jnp.zeros((), BF16)), xs, b, r, 0)
            return carry

        lax.fori_loop(0, 4, prep, 0)

    def tap_row(ref, dy):
        return ref[:, pl.ds(dy, 16)].reshape(1024, 1536)

    def conv_taps(h, dy, first):
        w_copy(h, dy).wait()
        part = nn(tap_row(xs, dy), wt[h, dy])
        if first:
            acc[...] = part
        else:
            acc[...] += part

    def finish_forward(h):
        pre = acc[...].astype(BF16)
        hp[h] = pre
        ht[0, h] = nt(perm[...], jnp.maximum(pre, jnp.zeros((), BF16))).astype(BF16)

    def hidden_back(h, k):
        rows = pl.ds(pl.multiple_of(k * 512, 512), 512)
        chans = pl.ds(pl.multiple_of(h * 256, 256), 256)
        back = nt(cot[rows], we[chans])
        hg[h, rows] = jnp.where(hp[h, rows].astype(F32) > 0, back, 0.0).astype(BF16)

    def finish_back(h):
        ht[1, h] = nt(perm[...], hg[h]).astype(BF16)

    def produce(p, k):
        q = 2 * p + k
        h = q // 13
        j = q % 13

        @pl.when(j < 4)
        def _():
            g = nn(ht[0, h], cot[:, pl.ds(pl.multiple_of(j * 512, 512), 512)]) * (1.0 / 1024.0)
            gm[q] = g.astype(BF16).reshape(4, 4, 16, 512)

        @pl.when(j >= 4)
        def _():
            t = j - 4
            at = pl.multiple_of((t % 3) * 512, 512)
            g = nn(ht[1, h], xs[:, pl.ds(t // 3, 16), :, pl.ds(at, 512)].reshape(1024, 512)) * (1.0 / 1024.0)
            gm[q] = g.astype(BF16).reshape(4, 4, 16, 512)

    def ring(k, stage):
        if (k + stage) % 2 == 0:
            return z, ((z + 1) % 4) * 4 + y, ((z + 3) % 4) * 4 + y
        return y, z * 4 + (y + 1) % 4, z * 4 + (y + 3) % 4

    def block(p, k, at):
        q = 2 * p + k
        return gm.at[q, at] if k == 0 else gm.at[q, :, at]

    def remote(src, dst, send, recv, inner):
        return pltpu.make_async_remote_copy(
            src_ref=src, dst_ref=dst, send_sem=send, recv_sem=recv,
            device_id={"inner": inner}, device_id_type=MESH,
        )

    LO, HI = slice(0, 256), slice(256, 512)

    def copies1(p, k):
        at, nxt, prv = ring(k, 0)
        far = block(p, k, (at + 2) % 4)
        return (
            remote(far.at[:, :, LO], r1p.at[p, k], s1p, q1p.at[p, k], nxt),
            remote(far.at[:, :, HI], r1m.at[p, k], s1m, q1m.at[p, k], prv),
        )

    def copies2(p, k):
        at, nxt, prv = ring(k, 0)
        return (
            remote(block(p, k, (at + 1) % 4), r2p.at[p, k], s2p, q2p.at[p, k], nxt),
            remote(block(p, k, (at + 3) % 4), r2m.at[p, k], s2m, q2m.at[p, k], prv),
        )

    def copies3(p, k):
        at, nxt, prv = ring(k, 1)
        far = tb.at[p, k, (at + 2) % 4]
        return (
            remote(far.at[:, LO], r3p.at[p, k], s3p, q3p.at[p, k], nxt),
            remote(far.at[:, HI], r3m.at[p, k], s3m, q3m.at[p, k], prv),
        )

    def copies4(p, k):
        at, nxt, prv = ring(k, 1)
        return (
            remote(tb.at[p, k, (at + 1) % 4], r4p.at[p, k], s4p, q4p.at[p, k], nxt),
            remote(tb.at[p, k, (at + 3) % 4], r4m.at[p, k], s4m, q4m.at[p, k], prv),
        )

    def step1(p, k):
        for c in copies1(p, k):
            c.start()

    def step2(p, k):
        at, _, _ = ring(k, 0)
        fwd, bwd = copies1(p, k)
        out_fwd, out_bwd = copies2(p, k)
        near = block(p, k, (at + 1) % 4)
        fwd.wait_recv()
        near[:, :, LO] = (near[:, :, LO].astype(F32) + r1p[p, k].astype(F32)).astype(BF16)
        out_fwd.start()
        near = block(p, k, (at + 3) % 4)
        bwd.wait_recv()
        near[:, :, HI] = (near[:, :, HI].astype(F32) + r1m[p, k].astype(F32)).astype(BF16)
        out_bwd.start()

    def step3(p, k):
        at, _, _ = ring(k, 0)
        for c in copies2(p, k):
            c.wait_recv()
        mine = block(p, k, at)
        total = mine[...].astype(F32) + r2p[p, k].astype(F32) + r2m[p, k].astype(F32)
        tb[p, k] = total.astype(BF16)
        for c in copies3(p, k):
            c.start()

    def step4(p, k):
        at, _, _ = ring(k, 1)
        fwd, bwd = copies3(p, k)
        out_fwd, out_bwd = copies4(p, k)
        near = tb.at[p, k, (at + 1) % 4]
        fwd.wait_recv()
        near[:, LO] = (near[:, LO].astype(F32) + r3p[p, k].astype(F32)).astype(BF16)
        out_fwd.start()
        near = tb.at[p, k, (at + 3) % 4]
        bwd.wait_recv()
        near[:, HI] = (near[:, HI].astype(F32) + r3m[p, k].astype(F32)).astype(BF16)
        out_bwd.start()

    def x_copy(p, k, part, j, dest):
        return pltpu.make_async_remote_copy(
            src_ref=ub.at[p, k, part], dst_ref=rx.at[j, o], send_sem=sx, recv_sem=qx.at[j],
            device_id={"outer": dest}, device_id_type=MESH,
        )

    def step5(p, k):
        at, _, _ = ring(k, 1)
        q = 2 * p + k
        h = q // 13
        j = q % 13
        for c in copies4(p, k):
            c.wait_recv()
        total = tb[p, k, at].astype(F32) + r4p[p, k].astype(F32) + r4m[p, k].astype(F32)
        for part in range(4):
            dest = h * 4 + part
            ub[p, k, part] = total[4 * part : 4 * part + 4]

            @pl.when(dest != o)
            def _():
                x_copy(p, k, part, j, dest).start()

            @pl.when(dest == o)
            def _():
                rx[j, o] = total[4 * part : 4 * part + 4]

    def step6(p, k):
        q = 2 * p + k
        j = q % 13

        @pl.when(q // 13 == o // 4)
        def _():
            pltpu.make_async_remote_copy(
                src_ref=rx.at[j, pl.ds(0, 7)], dst_ref=rx.at[j, pl.ds(0, 7)], send_sem=sx, recv_sem=qx.at[j],
                device_id={"outer": (o + 1) % 8}, device_id_type=MESH,
            ).wait_recv()
            kind = jnp.where(j < 4, 1, 0)
            vecs = [rx[j, a] for a in range(8)]
            for n, (a, b) in enumerate(GRAM):
                prod = vecs[a] * vecs[b]
                part = (prod[:, 0:128] + prod[:, 128:256]) + (prod[:, 256:384] + prod[:, 384:512])
                gacc[kind, n] = gacc[kind, n] + part

    for dy in range(3):
        conv_taps(0, dy, dy == 0)
    finish_forward(0)
    cot_copy.wait()
    we_copy.wait()
    pl.semaphore_wait(barrier, 22)

    def image_rows(g, carry):
        b, r = g // 4, g % 4
        rows = pl.ds(pl.multiple_of(g * 64, 64), 64)
        for h in range(2):
            spread(hg[h, rows], hs, b, r, h * 256)
        return carry

    def input_piece(ty, m):
        part = nt(hs[pl.ds(2 * m, 2), pl.ds(ty, 16)].reshape(512, 1536), wn[ty])
        rows = pl.ds(pl.multiple_of(512 * m, 512), 512)
        if ty == 0:
            acc2[rows] = part
        elif ty == 1:
            acc2[rows] += part
        else:
            images = pl.ds(2 * m, 2)
            total = acc2[rows] + part
            kept = jnp.where(xin[images].reshape(512, 512).astype(F32) > 0, total, 0.0)
            ig[images] = kept.astype(BF16).reshape(2, 16, 16, 512)

    def input_work(p):
        @pl.when(p == INPUT_AT - 1)
        def _():
            lax.fori_loop(0, 16, image_rows, 0)

        for ty in range(3):

            @pl.when(jnp.logical_and(p >= INPUT_AT + 2 * ty, p < INPUT_AT + 2 * ty + 2))
            def _():
                m = p - (INPUT_AT + 2 * ty)

                @pl.when(m == 0)
                def _():
                    for c in wn_copies(ty):
                        c.wait()

                input_piece(ty, m)

    def iteration(p, carry):
        for k in range(2):

            @pl.when(p < PAIRS)
            def _():
                produce(p, k)
                step1(p, k)

        for lag, step in ((LAG2, step2), (LAG3, step3), (LAG4, step4), (LAG5, step5), (LAG6, step6)):

            @pl.when(jnp.logical_and(p >= lag, p < PAIRS + lag))
            def _():
                for k in range(2):
                    step(p - lag, k)

        @pl.when(jnp.logical_or(p < 2, jnp.logical_or(p == 6, p == 7)))
        def _():
            h = p // 6
            hidden_back(h, p % 2)

            @pl.when(p % 2 == 1)
            def _():
                finish_back(h)

        @pl.when(p == 2)
        def _():
            conv_taps(1, 0, True)

        @pl.when(jnp.logical_or(p == 3, p == 4))
        def _():
            conv_taps(1, p - 2, False)

            @pl.when(p == 4)
            def _():
                finish_forward(1)

        input_work(p)
        return carry

    lax.fori_loop(0, PAIRS + LAG6, iteration, 0)

    lane = lax.broadcasted_iota(jnp.int32, (1, 128), 1)
    rows = []
    for kind in range(2):
        packed = jnp.zeros((1, 128), F32)
        for n in range(len(GRAM)):
            line = jnp.sum(gacc[kind, n], axis=0, keepdims=True)
            packed = jnp.where(lane == n, jnp.sum(line, axis=1, keepdims=True), packed)
        rows.append(packed)
    sub = lax.broadcasted_iota(jnp.int32, (8, 128), 0)
    mine = jnp.where(sub == 0, rows[0], jnp.where(sub == 1, rows[1], 0.0))

    def exchange(axis, me, count, value, src, dst, send, recv):
        src[...] = value
        dst[me] = value

        def go(d, carry):
            pltpu.make_async_remote_copy(
                src_ref=src, dst_ref=dst.at[me], send_sem=send, recv_sem=recv,
                device_id={axis: (me + d) % count}, device_id_type=MESH,
            ).start()
            return carry

        lax.fori_loop(1, count, go, 0)
        got = dst.at[pl.ds(0, count - 1)]
        pltpu.make_async_remote_copy(
            src_ref=got, dst_ref=got, send_sem=send, recv_sem=recv,
            device_id={axis: (me + 1) % count}, device_id_type=MESH,
        ).wait_recv()
        total = dst[0]
        for n in range(1, count):
            total = total + dst[n]
        return total

    total = exchange("outer", o, 8, mine, stat.at[0], st1, ss1, qs1)
    total = exchange("inner", i, 16, total, stat.at[1], st2, ss2, qs2)
    gram = {ab: jnp.broadcast_to(total[:, n : n + 1], (8, 128)) for ab, n in GRAM_AT.items()}
    weights = adasum_weights(gram)

    for kind, count, out in ((0, 9, fin_conv), (1, 4, fin_exp)):
        coef = [jnp.broadcast_to(jnp.tile(w[kind : kind + 1], (1, 4)), (4, 512)) for w in weights]
        for t in range(count):
            j = t if kind == 1 else t + 4
            value = coef[0] * rx[j, 0]
            for a in range(1, 8):
                value = value + coef[a] * rx[j, a]
            out[:, t * 512 : (t + 1) * 512] = value

    def drain(ref, send):
        pltpu.make_async_remote_copy(
            src_ref=ref, dst_ref=ref, send_sem=send, recv_sem=qs1,
            device_id={"outer": (o + 1) % 8}, device_id_type=MESH,
        ).wait_send()

    for ref, send in (
        (r1p, s1p), (r1m, s1m), (r2p, s2p), (r2m, s2m), (r3p, s3p), (r3m, s3m), (r4p, s4p), (r4m, s4m),
        (rx.at[:, pl.ds(0, 7)], sx), (st1.at[pl.ds(0, 7)], ss1), (st2.at[pl.ds(0, 15)], ss2),
    ):
        drain(ref, send)


def update_kernel(ig, fin_conv, fin_exp, mom_conv, mom_exp, ig_out, new_conv, new_exp, out_sem):
    copy = pltpu.make_async_copy(ig, ig_out, out_sem)
    copy.start()
    for fin, mom, new in ((fin_conv, mom_conv, new_conv), (fin_exp, mom_exp, new_exp)):
        n = fin.shape[1]
        for s in range(4):
            new[0:1, s * n : (s + 1) * n] = MOMENTUM * mom[0:1, s * n : (s + 1) * n] + fin[s : s + 1, :]
    copy.wait()


def body(inputs, cotangent, conv_weight, expand_weight, conv_momentum, expand_momentum):
    images, height, across, channels = inputs.shape
    rows = images * height * across
    dma = pltpu.SemaphoreType.DMA
    vmem = pltpu.VMEM
    any_spec = pl.BlockSpec(memory_space=pl.ANY)
    vmem_spec = pl.BlockSpec(memory_space=pltpu.VMEM)
    input_grad, fin_conv, fin_exp = pl.pallas_call(
        kernel,
        out_shape=(vmem(inputs.shape, BF16), vmem((4, 4608), F32), vmem((4, 2048), F32)),
        in_specs=[any_spec] * 4,
        out_specs=(vmem_spec, vmem_spec, vmem_spec),
        scratch_shapes=[
            vmem((4, 16, 16, 512), BF16),
            vmem((4, 18, 16, 1536), BF16),
            vmem((2, 3, 1536, 256), BF16),
            vmem((3, 512, 1536), BF16),
            vmem((512, 2048), BF16),
            vmem((1024, 2048), BF16),
            vmem((1024, 256), F32),
            vmem((2, 1024, 256), BF16),
            vmem((2, 2, 256, 1024), BF16),
            vmem((2, 1024, 256), BF16),
            vmem((4, 18, 16, 1536), BF16),
            vmem((1024, 512), F32),
            vmem((256, 256), BF16),
            vmem((26, 4, 4, 16, 512), BF16),
            vmem((PAIRS, 2, 4, 16, 256), BF16),
            vmem((PAIRS, 2, 4, 16, 256), BF16),
            vmem((PAIRS, 2, 4, 16, 512), BF16),
            vmem((PAIRS, 2, 4, 16, 512), BF16),
            vmem((PAIRS, 2, 4, 16, 512), BF16),
            vmem((PAIRS, 2, 16, 256), BF16),
            vmem((PAIRS, 2, 16, 256), BF16),
            vmem((PAIRS, 2, 16, 512), BF16),
            vmem((PAIRS, 2, 16, 512), BF16),
            vmem((PAIRS, 2, 4, 4, 512), F32),
            vmem((13, 8, 4, 512), F32),
            vmem((2, len(GRAM), 4, 128), F32),
            vmem((2, 8, 128), F32),
            vmem((8, 8, 128), F32),
            vmem((16, 8, 128), F32),
            dma((4,)), dma((2, 3)), dma((3, 3)), dma, dma,
        ]
        + [dma((PAIRS, 2))] * 8
        + [dma((13,)), dma, dma]
        + [dma] * 11,
        compiler_params=pltpu.CompilerParams(
            collective_id=0, has_side_effects=True, vmem_limit_bytes=VMEM_LIMIT
        ),
    )(inputs, cotangent.reshape(rows, cotangent.shape[-1]), conv_weight, expand_weight)
    return pl.pallas_call(
        update_kernel,
        out_shape=(
            jax.ShapeDtypeStruct(inputs.shape, BF16),
            jax.ShapeDtypeStruct(conv_momentum.shape, F32),
            jax.ShapeDtypeStruct(expand_momentum.shape, F32),
        ),
        in_specs=[vmem_spec] * 5,
        out_specs=(any_spec, vmem_spec, vmem_spec),
        scratch_shapes=[dma],
        compiler_params=pltpu.CompilerParams(vmem_limit_bytes=8 * 1024 * 1024),
    )(input_grad, fin_conv, fin_exp, conv_momentum, expand_momentum)


def solution(mesh):
    return jax.shard_map(
        body,
        mesh=mesh,
        in_specs=(
            P(("outer", "inner"), None, None, None),
            P(("outer", "inner"), None, None, None),
            P(),
            P(),
            P(("outer", "inner"), None),
            P(("outer", "inner"), None),
        ),
        out_specs=(
            P(("outer", "inner"), None, None, None),
            P(("outer", "inner"), None),
            P(("outer", "inner"), None),
        ),
        check_vma=False,
    )
```

```python
import jax
import jax.numpy as jnp
from jax import lax
from jax.experimental import pallas as pl
from jax.experimental.pallas import tpu as pltpu
from jax.sharding import PartitionSpec as P

EPS = 1e-06
MOMENTUM = 0.9
F32 = jnp.float32
BF16 = jnp.bfloat16
MESH = pl.DeviceIdType.MESH

PAIRS = 13
LAG2, LAG3, LAG4, LAG5, LAG6 = 2, 4, 6, 8, 13
INPUT_AT = 9
VMEM_LIMIT = 56 * 1024 * 1024
GRAM = [(a, b) for a in range(8) for b in range(a, 8)]
GRAM_AT = {ab: n for n, ab in enumerate(GRAM)}


def nn(a, b):
    return lax.dot_general(a, b, (((1,), (0,)), ((), ())), preferred_element_type=F32)


def nt(a, b):
    return lax.dot_general(a, b, (((1,), (1,)), ((), ())), preferred_element_type=F32)


def adasum_weights(gram):
    count = 8
    weights = [None] * 8
    span = 1
    while count > 1:
        coefs = []
        for m in range(count // 2):
            a, b = 2 * m, 2 * m + 1
            dot = gram[(a, b)]
            coefs.append(
                (
                    1.0 - dot / (2.0 * (gram[(a, a)] + EPS)),
                    1.0 - dot / (2.0 * (gram[(b, b)] + EPS)),
                )
            )
        merged = {}
        for m in range(count // 2):
            for n in range(m, count // 2):
                total = None
                for s in range(2):
                    for t in range(2):
                        key = (min(2 * m + s, 2 * n + t), max(2 * m + s, 2 * n + t))
                        term = coefs[m][s] * coefs[n][t] * gram[key]
                        total = term if total is None else total + term
                merged[(m, n)] = jnp.maximum(total, 0.0) if m == n else total
        for o in range(8):
            group = o // span
            c = coefs[group // 2][group % 2]
            weights[o] = c if weights[o] is None else weights[o] * c
        gram = merged
        count //= 2
        span *= 2
    return weights


def kernel(
    x_hbm, cot_hbm, w_hbm, we_hbm,
    ig, fin_conv, fin_exp,
    xin, xs, wt, wn, we, cot, acc, hp, ht, hg, hs, acc2, perm,
    gm, r1p, r1m, r2p, r2m, tb, r3p, r3m, r4p, r4m, ub, rx, gacc, stat, st1, st2,
    in_sem, w_sem, wn_sem, we_sem, cot_sem,
    q1p, q1m, q2p, q2m, q3p, q3m, q4p, q4m, qx, qs1, qs2,
    s1p, s1m, s2p, s2m, s3p, s3m, s4p, s4m, sx, ss1, ss2,
):
    o = lax.axis_index("outer")
    i = lax.axis_index("inner")
    z = i // 4
    y = i % 4

    barrier = pltpu.get_barrier_semaphore()

    def greet_outer(d, carry):
        pl.semaphore_signal(barrier, inc=1, device_id={"outer": (o + d) % 8}, device_id_type=MESH)
        return carry

    def greet_inner(d, carry):
        pl.semaphore_signal(barrier, inc=1, device_id={"inner": (i + d) % 16}, device_id_type=MESH)
        return carry

    lax.fori_loop(1, 8, greet_outer, 0)
    lax.fori_loop(1, 16, greet_inner, 0)

    def w_copy(h, dy):
        return pltpu.make_async_copy(
            w_hbm.at[pl.ds(dy * 1536, 1536), pl.ds(h * 256, 256)], wt.at[h, dy], w_sem.at[h, dy]
        )

    def wn_copies(ty):
        return [
            pltpu.make_async_copy(
                w_hbm.at[pl.ds(((2 - ty) * 3 + 2 - tx) * 512, 512)],
                wn.at[ty, :, pl.ds(tx * 512, 512)],
                wn_sem.at[ty, tx],
            )
            for tx in range(3)
        ]

    cot_copy = pltpu.make_async_copy(cot_hbm, cot, cot_sem)
    we_copy = pltpu.make_async_copy(we_hbm, we, we_sem)
    in_copies = [pltpu.make_async_copy(x_hbm.at[b], xin.at[b], in_sem.at[b]) for b in range(4)]
    for c in in_copies:
        c.start()
    for dy in range(3):
        w_copy(0, dy).start()
    cot_copy.start()
    we_copy.start()
    for dy in range(3):
        w_copy(1, dy).start()
    for ty in range(3):
        for c in wn_copies(ty):
            c.start()

    row = lax.broadcasted_iota(jnp.int32, (256, 256), 0)
    col = lax.broadcasted_iota(jnp.int32, (256, 256), 1)
    want = ((row // 4) % 4) * 64 + (row // 16) * 4 + row % 4
    perm[...] = jnp.where(want == col, 1.0, 0.0).astype(BF16)

    zero_row = jnp.zeros((16, 1536), BF16)
    for dst in (xs, hs):
        for b in range(4):
            dst[b, 0] = zero_row
            dst[b, 17] = zero_row
    gacc[...] = jnp.zeros_like(gacc)

    def spread(value, dst, b, r, first):
        n = value.shape[1]
        w = lax.broadcasted_iota(jnp.int32, (64, n), 0) % 16
        wide = value.astype(F32)
        left = jnp.where(w == 0, 0.0, pltpu.roll(wide, 1, 0)).astype(BF16)
        right = jnp.where(w == 15, 0.0, pltpu.roll(wide, 63, 0)).astype(BF16)
        for dx, v in ((0, left), (1, value), (2, right)):
            at = dx * 512 + first
            dst[b, pl.ds(1 + 4 * r, 4), :, at : at + n] = v.reshape(4, 16, n)


    for b in range(4):
        in_copies[b].wait()

        def prep(r, carry, b=b):
            v = xin[b, pl.ds(4 * r, 4)].reshape(64, 512)
            spread(jnp.maximum(v, jnp.zeros((), BF16)), xs, b, r, 0)
            return carry

        lax.fori_loop(0, 4, prep, 0)

    def tap_row(ref, dy):
        return ref[:, pl.ds(dy, 16)].reshape(1024, 1536)

    def conv_taps(h, dy, first):
        w_copy(h, dy).wait()
        part = nn(tap_row(xs, dy), wt[h, dy])
        if first:
            acc[...] = part
        else:
            acc[...] += part

    def finish_forward(h):
        pre = acc[...].astype(BF16)
        hp[h] = pre
        ht[0, h] = nt(perm[...], jnp.maximum(pre, jnp.zeros((), BF16))).astype(BF16)

    def hidden_back(h, k):
        rows = pl.ds(pl.multiple_of(k * 512, 512), 512)
        chans = pl.ds(pl.multiple_of(h * 256, 256), 256)
        back = nt(cot[rows], we[chans])
        hg[h, rows] = jnp.where(hp[h, rows].astype(F32) > 0, back, 0.0).astype(BF16)

    def finish_back(h):
        ht[1, h] = nt(perm[...], hg[h]).astype(BF16)

    def produce(p, k):
        q = 2 * p + k
        h = q // 13
        j = q % 13

        @pl.when(j < 4)
        def _():
            g = nn(ht[0, h], cot[:, pl.ds(pl.multiple_of(j * 512, 512), 512)]) * (1.0 / 1024.0)
            gm[q] = g.astype(BF16).reshape(4, 4, 16, 512)

        @pl.when(j >= 4)
        def _():
            t = j - 4
            at = pl.multiple_of((t % 3) * 512, 512)
            g = nn(ht[1, h], xs[:, pl.ds(t // 3, 16), :, pl.ds(at, 512)].reshape(1024, 512)) * (1.0 / 1024.0)
            gm[q] = g.astype(BF16).reshape(4, 4, 16, 512)

    def ring(k, stage):
        if (k + stage) % 2 == 0:
            return z, ((z + 1) % 4) * 4 + y, ((z + 3) % 4) * 4 + y
        return y, z * 4 + (y + 1) % 4, z * 4 + (y + 3) % 4

    def opposite(k):
        return z * 4 + (y + 2) % 4 if k == 0 else ((z + 2) % 4) * 4 + y

    def block(p, k, at):
        q = 2 * p + k
        return gm.at[q, at] if k == 0 else gm.at[q, :, at]

    def remote(src, dst, send, recv, inner):
        return pltpu.make_async_remote_copy(
            src_ref=src, dst_ref=dst, send_sem=send, recv_sem=recv,
            device_id={"inner": inner}, device_id_type=MESH,
        )

    LO, HI = slice(0, 256), slice(256, 512)

    def copies1(p, k):
        at, nxt, prv = ring(k, 0)
        far = block(p, k, (at + 2) % 4)
        return (
            remote(far.at[:, :, LO], r1p.at[p, k], s1p, q1p.at[p, k], nxt),
            remote(far.at[:, :, HI], r1m.at[p, k], s1m, q1m.at[p, k], prv),
        )

    def copies2(p, k):
        at, nxt, prv = ring(k, 0)
        return (
            remote(block(p, k, (at + 1) % 4), r2p.at[p, k], s2p, q2p.at[p, k], nxt),
            remote(block(p, k, (at + 3) % 4), r2m.at[p, k], s2m, q2m.at[p, k], prv),
        )

    def copies3(p, k, last=False):
        at, nxt, prv = ring(k, 1)
        if last:
            nxt = prv = opposite(k)
        far = tb.at[p, k, (at + 2) % 4]
        return (
            remote(far.at[:, LO], r3p.at[p, k], s3p, q3p.at[p, k], nxt),
            remote(far.at[:, HI], r3m.at[p, k], s3m, q3m.at[p, k], prv),
        )

    def copies4(p, k):
        at, nxt, prv = ring(k, 1)
        return (
            remote(tb.at[p, k, (at + 1) % 4], r4p.at[p, k], s4p, q4p.at[p, k], nxt),
            remote(tb.at[p, k, (at + 3) % 4], r4m.at[p, k], s4m, q4m.at[p, k], prv),
        )

    def step1(p, k):
        for c in copies1(p, k):
            c.start()

    def step2(p, k):
        at, _, _ = ring(k, 0)
        fwd, bwd = copies1(p, k)
        out_fwd, out_bwd = copies2(p, k)
        near = block(p, k, (at + 1) % 4)
        fwd.wait_recv()
        near[:, :, LO] = (near[:, :, LO].astype(F32) + r1p[p, k].astype(F32)).astype(BF16)
        out_fwd.start()
        near = block(p, k, (at + 3) % 4)
        bwd.wait_recv()
        near[:, :, HI] = (near[:, :, HI].astype(F32) + r1m[p, k].astype(F32)).astype(BF16)
        out_bwd.start()

    def step3(p, k):
        at, _, _ = ring(k, 0)
        for c in copies2(p, k):
            c.wait_recv()
        mine = block(p, k, at)
        total = mine[...].astype(F32) + r2p[p, k].astype(F32) + r2m[p, k].astype(F32)
        tb[p, k] = total.astype(BF16)

        @pl.when(p < PAIRS - 1)
        def _():
            for c in copies3(p, k):
                c.start()

        @pl.when(p == PAIRS - 1)
        def _():
            for c in copies3(p, k, last=True) + copies4(p, k):
                c.start()

    def step4(p, k):
        @pl.when(p < PAIRS - 1)
        def _():
            at, _, _ = ring(k, 1)
            fwd, bwd = copies3(p, k)
            out_fwd, out_bwd = copies4(p, k)
            near = tb.at[p, k, (at + 1) % 4]
            fwd.wait_recv()
            near[:, LO] = (near[:, LO].astype(F32) + r3p[p, k].astype(F32)).astype(BF16)
            out_fwd.start()
            near = tb.at[p, k, (at + 3) % 4]
            bwd.wait_recv()
            near[:, HI] = (near[:, HI].astype(F32) + r3m[p, k].astype(F32)).astype(BF16)
            out_bwd.start()

    def x_copy(p, k, part, j, dest):
        return pltpu.make_async_remote_copy(
            src_ref=ub.at[p, k, part], dst_ref=rx.at[j, o], send_sem=sx, recv_sem=qx.at[j],
            device_id={"outer": dest}, device_id_type=MESH,
        )

    def step5(p, k):
        at, _, _ = ring(k, 1)
        q = 2 * p + k
        h = q // 13
        j = q % 13
        for c in copies4(p, k):
            c.wait_recv()
        tail = tb.at[p, k, at]

        @pl.when(p == PAIRS - 1)
        def _():
            for c in copies3(p, k, last=True):
                c.wait_recv()
            tail[:, LO] = (tail[:, LO].astype(F32) + r3p[p, k].astype(F32)).astype(BF16)
            tail[:, HI] = (tail[:, HI].astype(F32) + r3m[p, k].astype(F32)).astype(BF16)

        total = tail[...].astype(F32) + r4p[p, k].astype(F32) + r4m[p, k].astype(F32)
        for part in range(4):
            dest = h * 4 + part
            ub[p, k, part] = total[4 * part : 4 * part + 4]

            @pl.when(dest != o)
            def _():
                x_copy(p, k, part, j, dest).start()

            @pl.when(dest == o)
            def _():
                rx[j, o] = total[4 * part : 4 * part + 4]

    def step6(p, k):
        q = 2 * p + k
        j = q % 13

        @pl.when(q // 13 == o // 4)
        def _():
            pltpu.make_async_remote_copy(
                src_ref=rx.at[j, pl.ds(0, 7)], dst_ref=rx.at[j, pl.ds(0, 7)], send_sem=sx, recv_sem=qx.at[j],
                device_id={"outer": (o + 1) % 8}, device_id_type=MESH,
            ).wait_recv()
            kind = jnp.where(j < 4, 1, 0)
            vecs = [rx[j, a] for a in range(8)]
            for n, (a, b) in enumerate(GRAM):
                prod = vecs[a] * vecs[b]
                part = (prod[:, 0:128] + prod[:, 128:256]) + (prod[:, 256:384] + prod[:, 384:512])
                gacc[kind, n] = gacc[kind, n] + part

    for dy in range(3):
        conv_taps(0, dy, dy == 0)
    finish_forward(0)
    cot_copy.wait()
    we_copy.wait()
    pl.semaphore_wait(barrier, 22)

    def image_rows(g, carry):
        b, r = g // 4, g % 4
        rows = pl.ds(pl.multiple_of(g * 64, 64), 64)
        for h in range(2):
            spread(hg[h, rows], hs, b, r, h * 256)
        return carry

    def input_piece(ty, m):
        part = nt(hs[pl.ds(2 * m, 2), pl.ds(ty, 16)].reshape(512, 1536), wn[ty])
        rows = pl.ds(pl.multiple_of(512 * m, 512), 512)
        if ty == 0:
            acc2[rows] = part
        elif ty == 1:
            acc2[rows] += part
        else:
            images = pl.ds(2 * m, 2)
            total = acc2[rows] + part
            kept = jnp.where(xin[images].reshape(512, 512).astype(F32) > 0, total, 0.0)
            ig[images] = kept.astype(BF16).reshape(2, 16, 16, 512)

    def input_work(p):
        @pl.when(p == INPUT_AT - 1)
        def _():
            lax.fori_loop(0, 16, image_rows, 0)

        for ty in range(3):

            @pl.when(jnp.logical_and(p >= INPUT_AT + 2 * ty, p < INPUT_AT + 2 * ty + 2))
            def _():
                m = p - (INPUT_AT + 2 * ty)

                @pl.when(m == 0)
                def _():
                    for c in wn_copies(ty):
                        c.wait()

                input_piece(ty, m)

    def iteration(p, carry):
        for k in range(2):

            @pl.when(p < PAIRS)
            def _():
                produce(p, k)
                step1(p, k)

        for lag, step in ((LAG2, step2), (LAG3, step3), (LAG4, step4), (LAG5, step5), (LAG6, step6)):

            @pl.when(jnp.logical_and(p >= lag, p < PAIRS + lag))
            def _():
                for k in range(2):
                    step(p - lag, k)

        @pl.when(jnp.logical_or(p < 2, jnp.logical_or(p == 6, p == 7)))
        def _():
            h = p // 6
            hidden_back(h, p % 2)

            @pl.when(p % 2 == 1)
            def _():
                finish_back(h)

        @pl.when(p == 2)
        def _():
            conv_taps(1, 0, True)

        @pl.when(jnp.logical_or(p == 3, p == 4))
        def _():
            conv_taps(1, p - 2, False)

            @pl.when(p == 4)
            def _():
                finish_forward(1)

        input_work(p)
        return carry

    lax.fori_loop(0, PAIRS + LAG6, iteration, 0)

    lane = lax.broadcasted_iota(jnp.int32, (1, 128), 1)
    rows = []
    for kind in range(2):
        packed = jnp.zeros((1, 128), F32)
        for n in range(len(GRAM)):
            line = jnp.sum(gacc[kind, n], axis=0, keepdims=True)
            packed = jnp.where(lane == n, jnp.sum(line, axis=1, keepdims=True), packed)
        rows.append(packed)
    sub = lax.broadcasted_iota(jnp.int32, (2, 128), 0)
    mine = jnp.where(sub == 0, rows[0], rows[1])

    def exchange(axis, me, count, value, src, dst, send, recv):
        src[...] = value
        dst[me] = value

        def go(d, carry):
            pltpu.make_async_remote_copy(
                src_ref=src, dst_ref=dst.at[me], send_sem=send, recv_sem=recv,
                device_id={axis: (me + d) % count}, device_id_type=MESH,
            ).start()
            return carry

        lax.fori_loop(1, count, go, 0)
        got = dst.at[pl.ds(0, count - 1)]
        pltpu.make_async_remote_copy(
            src_ref=got, dst_ref=got, send_sem=send, recv_sem=recv,
            device_id={axis: (me + 1) % count}, device_id_type=MESH,
        ).wait_recv()
        total = dst[0]
        for n in range(1, count):
            total = total + dst[n]
        return total

    total = exchange("outer", o, 8, mine, stat.at[0], st1, ss1, qs1)
    total = exchange("inner", i, 16, total, stat.at[1], st2, ss2, qs2)
    gram = {ab: jnp.broadcast_to(total[:, n : n + 1], (2, 128)) for ab, n in GRAM_AT.items()}
    weights = adasum_weights(gram)

    for kind, count, out in ((0, 9, fin_conv), (1, 4, fin_exp)):
        coef = [jnp.broadcast_to(jnp.tile(w[kind : kind + 1], (1, 4)), (4, 512)) for w in weights]
        for t in range(count):
            j = t if kind == 1 else t + 4
            value = coef[0] * rx[j, 0]
            for a in range(1, 8):
                value = value + coef[a] * rx[j, a]
            out[:, t * 512 : (t + 1) * 512] = value

    def drain(ref, send):
        pltpu.make_async_remote_copy(
            src_ref=ref, dst_ref=ref, send_sem=send, recv_sem=qs1,
            device_id={"outer": (o + 1) % 8}, device_id_type=MESH,
        ).wait_send()

    for ref, send in (
        (r1p, s1p), (r1m, s1m), (r2p, s2p), (r2m, s2m), (r3p, s3p), (r3m, s3m), (r4p, s4p), (r4m, s4m),
        (rx.at[:, pl.ds(0, 7)], sx), (st1.at[pl.ds(0, 7)], ss1), (st2.at[pl.ds(0, 15)], ss2),
    ):
        drain(ref, send)


def update_kernel(ig, fin_conv, fin_exp, mom_conv, mom_exp, ig_out, new_conv, new_exp, out_sem):
    copy = pltpu.make_async_copy(ig, ig_out, out_sem)
    copy.start()
    for fin, mom, new in ((fin_conv, mom_conv, new_conv), (fin_exp, mom_exp, new_exp)):
        n = fin.shape[1]
        for s in range(4):
            new[0:1, s * n : (s + 1) * n] = MOMENTUM * mom[0:1, s * n : (s + 1) * n] + fin[s : s + 1, :]
    copy.wait()


def body(inputs, cotangent, conv_weight, expand_weight, conv_momentum, expand_momentum):
    images, height, across, channels = inputs.shape
    rows = images * height * across
    dma = pltpu.SemaphoreType.DMA
    vmem = pltpu.VMEM
    any_spec = pl.BlockSpec(memory_space=pl.ANY)
    vmem_spec = pl.BlockSpec(memory_space=pltpu.VMEM)
    input_grad, fin_conv, fin_exp = pl.pallas_call(
        kernel,
        out_shape=(vmem(inputs.shape, BF16), vmem((4, 4608), F32), vmem((4, 2048), F32)),
        in_specs=[any_spec] * 4,
        out_specs=(vmem_spec, vmem_spec, vmem_spec),
        scratch_shapes=[
            vmem((4, 16, 16, 512), BF16),
            vmem((4, 18, 16, 1536), BF16),
            vmem((2, 3, 1536, 256), BF16),
            vmem((3, 512, 1536), BF16),
            vmem((512, 2048), BF16),
            vmem((1024, 2048), BF16),
            vmem((1024, 256), F32),
            vmem((2, 1024, 256), BF16),
            vmem((2, 2, 256, 1024), BF16),
            vmem((2, 1024, 256), BF16),
            vmem((4, 18, 16, 1536), BF16),
            vmem((1024, 512), F32),
            vmem((256, 256), BF16),
            vmem((26, 4, 4, 16, 512), BF16),
            vmem((PAIRS, 2, 4, 16, 256), BF16),
            vmem((PAIRS, 2, 4, 16, 256), BF16),
            vmem((PAIRS, 2, 4, 16, 512), BF16),
            vmem((PAIRS, 2, 4, 16, 512), BF16),
            vmem((PAIRS, 2, 4, 16, 512), BF16),
            vmem((PAIRS, 2, 16, 256), BF16),
            vmem((PAIRS, 2, 16, 256), BF16),
            vmem((PAIRS, 2, 16, 512), BF16),
            vmem((PAIRS, 2, 16, 512), BF16),
            vmem((PAIRS, 2, 4, 4, 512), F32),
            vmem((13, 8, 4, 512), F32),
            vmem((2, len(GRAM), 4, 128), F32),
            vmem((2, 2, 128), F32),
            vmem((8, 2, 128), F32),
            vmem((16, 2, 128), F32),
            dma((4,)), dma((2, 3)), dma((3, 3)), dma, dma,
        ]
        + [dma((PAIRS, 2))] * 8
        + [dma((13,)), dma, dma]
        + [dma] * 11,
        compiler_params=pltpu.CompilerParams(
            collective_id=0, has_side_effects=True, vmem_limit_bytes=VMEM_LIMIT
        ),
    )(inputs, cotangent.reshape(rows, cotangent.shape[-1]), conv_weight, expand_weight)
    return pl.pallas_call(
        update_kernel,
        out_shape=(
            jax.ShapeDtypeStruct(inputs.shape, BF16),
            jax.ShapeDtypeStruct(conv_momentum.shape, F32),
            jax.ShapeDtypeStruct(expand_momentum.shape, F32),
        ),
        in_specs=[vmem_spec] * 5,
        out_specs=(any_spec, vmem_spec, vmem_spec),
        scratch_shapes=[dma],
        compiler_params=pltpu.CompilerParams(vmem_limit_bytes=8 * 1024 * 1024),
    )(input_grad, fin_conv, fin_exp, conv_momentum, expand_momentum)


def solution(mesh):
    return jax.shard_map(
        body,
        mesh=mesh,
        in_specs=(
            P(("outer", "inner"), None, None, None),
            P(("outer", "inner"), None, None, None),
            P(),
            P(),
            P(("outer", "inner"), None),
            P(("outer", "inner"), None),
        ),
        out_specs=(
            P(("outer", "inner"), None, None, None),
            P(("outer", "inner"), None),
            P(("outer", "inner"), None),
        ),
        check_vma=False,
    )
```

```python
import jax
import jax.numpy as jnp
from jax import lax
from jax.experimental import pallas as pl
from jax.experimental.pallas import tpu as pltpu
from jax.sharding import PartitionSpec as P

EPS = 1e-06
MOMENTUM = 0.9
F32 = jnp.float32
BF16 = jnp.bfloat16
MESH = pl.DeviceIdType.MESH

PAIRS = 13
LAG2, LAG3, LAG4, LAG5, LAG6 = 2, 4, 6, 8, 13
INPUT_AT = 9
VMEM_LIMIT = 56 * 1024 * 1024
GRAM = [(a, b) for a in range(8) for b in range(a, 8)]
GRAM_AT = {ab: n for n, ab in enumerate(GRAM)}


def nn(a, b):
    return lax.dot_general(a, b, (((1,), (0,)), ((), ())), preferred_element_type=F32)


def nt(a, b):
    return lax.dot_general(a, b, (((1,), (1,)), ((), ())), preferred_element_type=F32)


def adasum_weights(gram):
    count = 8
    weights = [None] * 8
    span = 1
    while count > 1:
        coefs = []
        for m in range(count // 2):
            a, b = 2 * m, 2 * m + 1
            dot = gram[(a, b)]
            coefs.append(
                (
                    1.0 - dot / (2.0 * (gram[(a, a)] + EPS)),
                    1.0 - dot / (2.0 * (gram[(b, b)] + EPS)),
                )
            )
        merged = {}
        for m in range(count // 2):
            for n in range(m, count // 2):
                total = None
                for s in range(2):
                    for t in range(2):
                        key = (min(2 * m + s, 2 * n + t), max(2 * m + s, 2 * n + t))
                        term = coefs[m][s] * coefs[n][t] * gram[key]
                        total = term if total is None else total + term
                merged[(m, n)] = jnp.maximum(total, 0.0) if m == n else total
        for o in range(8):
            group = o // span
            c = coefs[group // 2][group % 2]
            weights[o] = c if weights[o] is None else weights[o] * c
        gram = merged
        count //= 2
        span *= 2
    return weights


def kernel(
    x_hbm, cot_hbm, w_hbm, we_hbm,
    ig, fin_conv, fin_exp,
    xin, xs, wt, wn, we, cot, acc, hp, ht, hg, hs, acc2, perm,
    gm, r1p, r1m, r2p, r2m, tb, r3p, r3m, r4p, r4m, ub, rx, gacc, stat, st1, st2,
    in_sem, w_sem, wn_sem, we_sem, cot_sem,
    q1p, q1m, q2p, q2m, q3p, q3m, q4p, q4m, qx, qs1, qs2,
    s1p, s1m, s2p, s2m, s3p, s3m, s4p, s4m, sx, ss1, ss2,
):
    o = lax.axis_index("outer")
    i = lax.axis_index("inner")
    z = i // 4
    y = i % 4

    barrier = pltpu.get_barrier_semaphore()

    def greet_outer(d, carry):
        pl.semaphore_signal(barrier, inc=1, device_id={"outer": (o + d) % 8}, device_id_type=MESH)
        return carry

    def greet_inner(d, carry):
        pl.semaphore_signal(barrier, inc=1, device_id={"inner": (i + d) % 16}, device_id_type=MESH)
        return carry

    lax.fori_loop(1, 8, greet_outer, 0)
    lax.fori_loop(1, 16, greet_inner, 0)

    def w_copy(h, dy):
        return pltpu.make_async_copy(
            w_hbm.at[pl.ds(dy * 1536, 1536), pl.ds(h * 256, 256)], wt.at[h, dy], w_sem.at[h, dy]
        )

    def wn_copies(ty):
        return [
            pltpu.make_async_copy(
                w_hbm.at[pl.ds(((2 - ty) * 3 + 2 - tx) * 512, 512)],
                wn.at[ty, :, pl.ds(tx * 512, 512)],
                wn_sem.at[ty, tx],
            )
            for tx in range(3)
        ]

    cot_copy = pltpu.make_async_copy(cot_hbm, cot, cot_sem)
    we_copy = pltpu.make_async_copy(we_hbm, we, we_sem)
    in_copies = [pltpu.make_async_copy(x_hbm.at[b], xin.at[b], in_sem.at[b]) for b in range(4)]
    for c in in_copies:
        c.start()
    for dy in range(3):
        w_copy(0, dy).start()
    cot_copy.start()
    we_copy.start()
    for dy in range(3):
        w_copy(1, dy).start()
    for ty in range(3):
        for c in wn_copies(ty):
            c.start()

    row = lax.broadcasted_iota(jnp.int32, (256, 256), 0)
    col = lax.broadcasted_iota(jnp.int32, (256, 256), 1)
    want = ((row // 4) % 4) * 64 + (row // 16) * 4 + row % 4
    perm[...] = jnp.where(want == col, 1.0, 0.0).astype(BF16)

    zero_row = jnp.zeros((16, 1536), BF16)
    for dst in (xs, hs):
        for b in range(4):
            dst[b, 0] = zero_row
            dst[b, 17] = zero_row
    gacc[...] = jnp.zeros_like(gacc)

    def spread(value, dst, b, r, first):
        n = value.shape[1]
        w = lax.broadcasted_iota(jnp.int32, (64, n), 0) % 16
        wide = value.astype(F32)
        left = jnp.where(w == 0, 0.0, pltpu.roll(wide, 1, 0)).astype(BF16)
        right = jnp.where(w == 15, 0.0, pltpu.roll(wide, 63, 0)).astype(BF16)
        for dx, v in ((0, left), (1, value), (2, right)):
            at = dx * 512 + first
            dst[b, pl.ds(1 + 4 * r, 4), :, at : at + n] = v.reshape(4, 16, n)


    for b in range(4):
        in_copies[b].wait()

        def prep(r, carry, b=b):
            v = xin[b, pl.ds(4 * r, 4)].reshape(64, 512)
            spread(jnp.maximum(v, jnp.zeros((), BF16)), xs, b, r, 0)
            return carry

        lax.fori_loop(0, 4, prep, 0)

    def tap_row(ref, dy):
        return ref[:, pl.ds(dy, 16)].reshape(1024, 1536)

    def conv_taps(h, dy, first):
        w_copy(h, dy).wait()
        part = nn(tap_row(xs, dy), wt[h, dy])
        if first:
            acc[...] = part
        else:
            acc[...] += part

    def finish_forward(h, total):
        pre = total.astype(BF16)
        hp[h] = pre
        ht[0, h] = nt(perm[...], jnp.maximum(pre, jnp.zeros((), BF16))).astype(BF16)

    def hidden_back(h, k):
        rows = pl.ds(pl.multiple_of(k * 512, 512), 512)
        chans = pl.ds(pl.multiple_of(h * 256, 256), 256)
        back = nt(cot[rows], we[chans])
        hg[h, rows] = jnp.where(hp[h, rows].astype(F32) > 0, back, 0.0).astype(BF16)

    def finish_back(h):
        ht[1, h] = nt(perm[...], hg[h]).astype(BF16)

    def produce(p, k):
        q = 2 * p + k
        h = q // 13
        j = q % 13

        @pl.when(j < 4)
        def _():
            g = nn(ht[0, h], cot[:, pl.ds(pl.multiple_of(j * 512, 512), 512)]) * (1.0 / 1024.0)
            gm[q] = g.astype(BF16).reshape(4, 4, 16, 512)

        @pl.when(j >= 4)
        def _():
            t = j - 4
            at = pl.multiple_of((t % 3) * 512, 512)
            g = nn(ht[1, h], xs[:, pl.ds(t // 3, 16), :, pl.ds(at, 512)].reshape(1024, 512)) * (1.0 / 1024.0)
            gm[q] = g.astype(BF16).reshape(4, 4, 16, 512)

    def ring(k, stage):
        if (k + stage) % 2 == 0:
            return z, ((z + 1) % 4) * 4 + y, ((z + 3) % 4) * 4 + y
        return y, z * 4 + (y + 1) % 4, z * 4 + (y + 3) % 4

    def opposite(k):
        return z * 4 + (y + 2) % 4 if k == 0 else ((z + 2) % 4) * 4 + y

    def block(p, k, at):
        q = 2 * p + k
        return gm.at[q, at] if k == 0 else gm.at[q, :, at]

    def remote(src, dst, send, recv, inner):
        return pltpu.make_async_remote_copy(
            src_ref=src, dst_ref=dst, send_sem=send, recv_sem=recv,
            device_id={"inner": inner}, device_id_type=MESH,
        )

    LO, HI = slice(0, 256), slice(256, 512)

    def copies1(p, k):
        at, nxt, prv = ring(k, 0)
        far = block(p, k, (at + 2) % 4)
        return (
            remote(far.at[:, :, LO], r1p.at[p, k], s1p, q1p.at[p, k], nxt),
            remote(far.at[:, :, HI], r1m.at[p, k], s1m, q1m.at[p, k], prv),
        )

    def copies2(p, k):
        at, nxt, prv = ring(k, 0)
        return (
            remote(block(p, k, (at + 1) % 4), r2p.at[p, k], s2p, q2p.at[p, k], nxt),
            remote(block(p, k, (at + 3) % 4), r2m.at[p, k], s2m, q2m.at[p, k], prv),
        )

    def copies3(p, k, last=False):
        at, nxt, prv = ring(k, 1)
        if last:
            nxt = prv = opposite(k)
        far = tb.at[p, k, (at + 2) % 4]
        return (
            remote(far.at[:, LO], r3p.at[p, k], s3p, q3p.at[p, k], nxt),
            remote(far.at[:, HI], r3m.at[p, k], s3m, q3m.at[p, k], prv),
        )

    def copies4(p, k):
        at, nxt, prv = ring(k, 1)
        return (
            remote(tb.at[p, k, (at + 1) % 4], r4p.at[p, k], s4p, q4p.at[p, k], nxt),
            remote(tb.at[p, k, (at + 3) % 4], r4m.at[p, k], s4m, q4m.at[p, k], prv),
        )

    def step1(p, k):
        for c in copies1(p, k):
            c.start()

    def step2(p, k):
        at, _, _ = ring(k, 0)
        fwd, bwd = copies1(p, k)
        out_fwd, out_bwd = copies2(p, k)
        near = block(p, k, (at + 1) % 4)
        fwd.wait_recv()
        near[:, :, LO] = (near[:, :, LO].astype(F32) + r1p[p, k].astype(F32)).astype(BF16)
        out_fwd.start()
        near = block(p, k, (at + 3) % 4)
        bwd.wait_recv()
        near[:, :, HI] = (near[:, :, HI].astype(F32) + r1m[p, k].astype(F32)).astype(BF16)
        out_bwd.start()

    def step3(p, k):
        at, _, _ = ring(k, 0)
        for c in copies2(p, k):
            c.wait_recv()
        mine = block(p, k, at)
        total = mine[...].astype(F32) + r2p[p, k].astype(F32) + r2m[p, k].astype(F32)
        tb[p, k] = total.astype(BF16)

        @pl.when(p < PAIRS - 1)
        def _():
            for c in copies3(p, k):
                c.start()

        @pl.when(p == PAIRS - 1)
        def _():
            for c in copies3(p, k, last=True) + copies4(p, k):
                c.start()

    def step4(p, k):
        @pl.when(p < PAIRS - 1)
        def _():
            at, _, _ = ring(k, 1)
            fwd, bwd = copies3(p, k)
            out_fwd, out_bwd = copies4(p, k)
            near = tb.at[p, k, (at + 1) % 4]
            fwd.wait_recv()
            near[:, LO] = (near[:, LO].astype(F32) + r3p[p, k].astype(F32)).astype(BF16)
            out_fwd.start()
            near = tb.at[p, k, (at + 3) % 4]
            bwd.wait_recv()
            near[:, HI] = (near[:, HI].astype(F32) + r3m[p, k].astype(F32)).astype(BF16)
            out_bwd.start()

    def x_copy(p, k, part, j, dest):
        return pltpu.make_async_remote_copy(
            src_ref=ub.at[p, k, part], dst_ref=rx.at[j, o], send_sem=sx, recv_sem=qx.at[j],
            device_id={"outer": dest}, device_id_type=MESH,
        )

    def step5(p, k):
        at, _, _ = ring(k, 1)
        q = 2 * p + k
        h = q // 13
        j = q % 13
        for c in copies4(p, k):
            c.wait_recv()
        tail = tb.at[p, k, at]

        @pl.when(p == PAIRS - 1)
        def _():
            for c in copies3(p, k, last=True):
                c.wait_recv()
            tail[:, LO] = (tail[:, LO].astype(F32) + r3p[p, k].astype(F32)).astype(BF16)
            tail[:, HI] = (tail[:, HI].astype(F32) + r3m[p, k].astype(F32)).astype(BF16)

        total = tail[...].astype(F32) + r4p[p, k].astype(F32) + r4m[p, k].astype(F32)
        for part in range(4):
            dest = h * 4 + part
            ub[p, k, part] = total[4 * part : 4 * part + 4]

            @pl.when(dest != o)
            def _():
                x_copy(p, k, part, j, dest).start()

            @pl.when(dest == o)
            def _():
                rx[j, o] = total[4 * part : 4 * part + 4]

    def step6(p, k):
        q = 2 * p + k
        j = q % 13

        @pl.when(q // 13 == o // 4)
        def _():
            pltpu.make_async_remote_copy(
                src_ref=rx.at[j, pl.ds(0, 7)], dst_ref=rx.at[j, pl.ds(0, 7)], send_sem=sx, recv_sem=qx.at[j],
                device_id={"outer": (o + 1) % 8}, device_id_type=MESH,
            ).wait_recv()
            kind = jnp.where(j < 4, 1, 0)
            vecs = [rx[j, a] for a in range(8)]
            for n, (a, b) in enumerate(GRAM):
                prod = vecs[a] * vecs[b]
                part = (prod[:, 0:128] + prod[:, 128:256]) + (prod[:, 256:384] + prod[:, 384:512])
                gacc[kind, n] = gacc[kind, n] + part

    for dy in range(3):
        w_copy(0, dy).wait()
    finish_forward(0, nn(tap_row(xs, 0), wt[0, 0]) + nn(tap_row(xs, 1), wt[0, 1]) + nn(tap_row(xs, 2), wt[0, 2]))
    cot_copy.wait()
    we_copy.wait()
    pl.semaphore_wait(barrier, 22)

    def image_rows(g, carry):
        b, r = g // 4, g % 4
        rows = pl.ds(pl.multiple_of(g * 64, 64), 64)
        for h in range(2):
            spread(hg[h, rows], hs, b, r, h * 256)
        return carry

    def input_piece(ty, m):
        part = nt(hs[pl.ds(2 * m, 2), pl.ds(ty, 16)].reshape(512, 1536), wn[ty])
        rows = pl.ds(pl.multiple_of(512 * m, 512), 512)
        if ty == 0:
            acc2[rows] = part
        elif ty == 1:
            acc2[rows] += part
        else:
            images = pl.ds(2 * m, 2)
            total = acc2[rows] + part
            kept = jnp.where(xin[images].reshape(512, 512).astype(F32) > 0, total, 0.0)
            ig[images] = kept.astype(BF16).reshape(2, 16, 16, 512)

    def input_work(p):
        @pl.when(p == INPUT_AT - 1)
        def _():
            lax.fori_loop(0, 16, image_rows, 0)

        for ty in range(3):

            @pl.when(jnp.logical_and(p >= INPUT_AT + 2 * ty, p < INPUT_AT + 2 * ty + 2))
            def _():
                m = p - (INPUT_AT + 2 * ty)

                @pl.when(m == 0)
                def _():
                    for c in wn_copies(ty):
                        c.wait()

                input_piece(ty, m)

    def iteration(p, carry):
        for k in range(2):

            @pl.when(p < PAIRS)
            def _():
                produce(p, k)
                step1(p, k)

        for lag, step in ((LAG2, step2), (LAG3, step3), (LAG4, step4), (LAG5, step5), (LAG6, step6)):

            @pl.when(jnp.logical_and(p >= lag, p < PAIRS + lag))
            def _():
                for k in range(2):
                    step(p - lag, k)

        @pl.when(jnp.logical_or(p < 2, jnp.logical_or(p == 6, p == 7)))
        def _():
            h = p // 6
            hidden_back(h, p % 2)

            @pl.when(p % 2 == 1)
            def _():
                finish_back(h)

        @pl.when(p == 2)
        def _():
            conv_taps(1, 0, True)

        @pl.when(jnp.logical_or(p == 3, p == 4))
        def _():
            conv_taps(1, p - 2, False)

            @pl.when(p == 4)
            def _():
                finish_forward(1, acc[...])

        input_work(p)
        return carry

    lax.fori_loop(0, PAIRS + LAG6, iteration, 0)

    lane = lax.broadcasted_iota(jnp.int32, (1, 128), 1)
    rows = []
    for kind in range(2):
        packed = jnp.zeros((1, 128), F32)
        for n in range(len(GRAM)):
            line = jnp.sum(gacc[kind, n], axis=0, keepdims=True)
            packed = jnp.where(lane == n, jnp.sum(line, axis=1, keepdims=True), packed)
        rows.append(packed)
    sub = lax.broadcasted_iota(jnp.int32, (2, 128), 0)
    mine = jnp.where(sub == 0, rows[0], rows[1])

    def exchange(axis, me, count, value, src, dst, send, recv):
        src[...] = value
        dst[me] = value

        def go(d, carry):
            pltpu.make_async_remote_copy(
                src_ref=src, dst_ref=dst.at[me], send_sem=send, recv_sem=recv,
                device_id={axis: (me + d) % count}, device_id_type=MESH,
            ).start()
            return carry

        lax.fori_loop(1, count, go, 0)
        got = dst.at[pl.ds(0, count - 1)]
        pltpu.make_async_remote_copy(
            src_ref=got, dst_ref=got, send_sem=send, recv_sem=recv,
            device_id={axis: (me + 1) % count}, device_id_type=MESH,
        ).wait_recv()
        total = dst[0]
        for n in range(1, count):
            total = total + dst[n]
        return total

    total = exchange("outer", o, 8, mine, stat.at[0], st1, ss1, qs1)
    total = exchange("inner", i, 16, total, stat.at[1], st2, ss2, qs2)
    gram = {ab: jnp.broadcast_to(total[:, n : n + 1], (2, 128)) for ab, n in GRAM_AT.items()}
    weights = adasum_weights(gram)

    for kind, count, out in ((0, 9, fin_conv), (1, 4, fin_exp)):
        coef = [jnp.broadcast_to(jnp.tile(w[kind : kind + 1], (1, 4)), (4, 512)) for w in weights]
        for t in range(count):
            j = t if kind == 1 else t + 4
            value = coef[0] * rx[j, 0]
            for a in range(1, 8):
                value = value + coef[a] * rx[j, a]
            out[:, t * 512 : (t + 1) * 512] = value

    def drain(ref, send):
        pltpu.make_async_remote_copy(
            src_ref=ref, dst_ref=ref, send_sem=send, recv_sem=qs1,
            device_id={"outer": (o + 1) % 8}, device_id_type=MESH,
        ).wait_send()

    for ref, send in (
        (r1p, s1p), (r1m, s1m), (r2p, s2p), (r2m, s2m), (r3p, s3p), (r3m, s3m), (r4p, s4p), (r4m, s4m),
        (rx.at[:, pl.ds(0, 7)], sx), (st1.at[pl.ds(0, 7)], ss1), (st2.at[pl.ds(0, 15)], ss2),
    ):
        drain(ref, send)


def update_kernel(
    ig, fin_conv, fin_exp, mom_conv, mom_exp, ig_out, conv_out, exp_out, new_conv, new_exp, out_sem
):
    copies = [pltpu.make_async_copy(ig, ig_out, out_sem.at[0])]
    copies[0].start()
    for at, fin, mom, new, out in (
        (1, fin_conv, mom_conv, new_conv, conv_out), (2, fin_exp, mom_exp, new_exp, exp_out),
    ):
        n = fin.shape[1]
        for s in range(4):
            new[0:1, s * n : (s + 1) * n] = MOMENTUM * mom[0:1, s * n : (s + 1) * n] + fin[s : s + 1, :]
        copies.append(pltpu.make_async_copy(new, out, out_sem.at[at]))
        copies[-1].start()
    for copy in copies:
        copy.wait()


def body(inputs, cotangent, conv_weight, expand_weight, conv_momentum, expand_momentum):
    images, height, across, channels = inputs.shape
    rows = images * height * across
    dma = pltpu.SemaphoreType.DMA
    vmem = pltpu.VMEM
    any_spec = pl.BlockSpec(memory_space=pl.ANY)
    vmem_spec = pl.BlockSpec(memory_space=pltpu.VMEM)
    input_grad, fin_conv, fin_exp = pl.pallas_call(
        kernel,
        out_shape=(vmem(inputs.shape, BF16), vmem((4, 4608), F32), vmem((4, 2048), F32)),
        in_specs=[any_spec] * 4,
        out_specs=(vmem_spec, vmem_spec, vmem_spec),
        scratch_shapes=[
            vmem((4, 16, 16, 512), BF16),
            vmem((4, 18, 16, 1536), BF16),
            vmem((2, 3, 1536, 256), BF16),
            vmem((3, 512, 1536), BF16),
            vmem((512, 2048), BF16),
            vmem((1024, 2048), BF16),
            vmem((1024, 256), F32),
            vmem((2, 1024, 256), BF16),
            vmem((2, 2, 256, 1024), BF16),
            vmem((2, 1024, 256), BF16),
            vmem((4, 18, 16, 1536), BF16),
            vmem((1024, 512), F32),
            vmem((256, 256), BF16),
            vmem((26, 4, 4, 16, 512), BF16),
            vmem((PAIRS, 2, 4, 16, 256), BF16),
            vmem((PAIRS, 2, 4, 16, 256), BF16),
            vmem((PAIRS, 2, 4, 16, 512), BF16),
            vmem((PAIRS, 2, 4, 16, 512), BF16),
            vmem((PAIRS, 2, 4, 16, 512), BF16),
            vmem((PAIRS, 2, 16, 256), BF16),
            vmem((PAIRS, 2, 16, 256), BF16),
            vmem((PAIRS, 2, 16, 512), BF16),
            vmem((PAIRS, 2, 16, 512), BF16),
            vmem((PAIRS, 2, 4, 4, 512), F32),
            vmem((13, 8, 4, 512), F32),
            vmem((2, len(GRAM), 4, 128), F32),
            vmem((2, 2, 128), F32),
            vmem((8, 2, 128), F32),
            vmem((16, 2, 128), F32),
            dma((4,)), dma((2, 3)), dma((3, 3)), dma, dma,
        ]
        + [dma((PAIRS, 2))] * 8
        + [dma((13,)), dma, dma]
        + [dma] * 11,
        compiler_params=pltpu.CompilerParams(
            collective_id=0, has_side_effects=True, vmem_limit_bytes=VMEM_LIMIT
        ),
    )(inputs, cotangent.reshape(rows, cotangent.shape[-1]), conv_weight, expand_weight)
    return pl.pallas_call(
        update_kernel,
        out_shape=(
            jax.ShapeDtypeStruct(inputs.shape, BF16),
            jax.ShapeDtypeStruct(conv_momentum.shape, F32),
            jax.ShapeDtypeStruct(expand_momentum.shape, F32),
        ),
        in_specs=[vmem_spec] * 5,
        out_specs=(any_spec,) * 3,
        scratch_shapes=[vmem(conv_momentum.shape, F32), vmem(expand_momentum.shape, F32), dma((3,))],
        compiler_params=pltpu.CompilerParams(vmem_limit_bytes=8 * 1024 * 1024),
    )(input_grad, fin_conv, fin_exp, conv_momentum, expand_momentum)


def solution(mesh):
    return jax.shard_map(
        body,
        mesh=mesh,
        in_specs=(
            P(("outer", "inner"), None, None, None),
            P(("outer", "inner"), None, None, None),
            P(),
            P(),
            P(("outer", "inner"), None),
            P(("outer", "inner"), None),
        ),
        out_specs=(
            P(("outer", "inner"), None, None, None),
            P(("outer", "inner"), None),
            P(("outer", "inner"), None),
        ),
        check_vma=False,
    )
```

```python
import jax
import jax.numpy as jnp
from jax import lax
from jax.experimental import pallas as pl
from jax.experimental.pallas import tpu as pltpu
from jax.sharding import PartitionSpec as P

EPS = 1e-06
MOMENTUM = 0.9
F32 = jnp.float32
BF16 = jnp.bfloat16
MESH = pl.DeviceIdType.MESH

PAIRS = 13
LAG2, LAG3, LAG4, LAG5, LAG6 = 2, 4, 6, 8, 13
INPUT_AT = 9
VMEM_LIMIT = 56 * 1024 * 1024
GRAM = [(a, b) for a in range(8) for b in range(a, 8)]
GRAM_AT = {ab: n for n, ab in enumerate(GRAM)}


def nn(a, b):
    return lax.dot_general(a, b, (((1,), (0,)), ((), ())), preferred_element_type=F32)


def nt(a, b):
    return lax.dot_general(a, b, (((1,), (1,)), ((), ())), preferred_element_type=F32)


def adasum_weights(gram):
    count = 8
    weights = [None] * 8
    span = 1
    while count > 1:
        coefs = []
        for m in range(count // 2):
            a, b = 2 * m, 2 * m + 1
            dot = gram[(a, b)]
            coefs.append(
                (
                    1.0 - dot / (2.0 * (gram[(a, a)] + EPS)),
                    1.0 - dot / (2.0 * (gram[(b, b)] + EPS)),
                )
            )
        merged = {}
        for m in range(count // 2):
            for n in range(m, count // 2):
                total = None
                for s in range(2):
                    for t in range(2):
                        key = (min(2 * m + s, 2 * n + t), max(2 * m + s, 2 * n + t))
                        term = coefs[m][s] * coefs[n][t] * gram[key]
                        total = term if total is None else total + term
                merged[(m, n)] = jnp.maximum(total, 0.0) if m == n else total
        for o in range(8):
            group = o // span
            c = coefs[group // 2][group % 2]
            weights[o] = c if weights[o] is None else weights[o] * c
        gram = merged
        count //= 2
        span *= 2
    return weights


def kernel(
    x_hbm, cot_hbm, w_hbm, we_hbm,
    ig, fin_conv, fin_exp,
    xin, xs, wt, wn, we, cot, acc, hp, ht, hg, hs, acc2, perm,
    gm, r1p, r1m, r2p, r2m, tb, r3p, r3m, r4p, r4m, ub, rx, gacc, stat, st1, st2,
    in_sem, w_sem, wn_sem, we_sem, cot_sem,
    q1p, q1m, q2p, q2m, q3p, q3m, q4p, q4m, qx, qs1, qs2,
    s1p, s1m, s2p, s2m, s3p, s3m, s4p, s4m, sx, ss1, ss2,
):
    o = lax.axis_index("outer")
    i = lax.axis_index("inner")
    z = i // 4
    y = i % 4

    barrier = pltpu.get_barrier_semaphore()

    def greet_outer(d, carry):
        pl.semaphore_signal(barrier, inc=1, device_id={"outer": (o + d) % 8}, device_id_type=MESH)
        return carry

    def greet_inner(d, carry):
        pl.semaphore_signal(barrier, inc=1, device_id={"inner": (i + d) % 16}, device_id_type=MESH)
        return carry

    def w_copy(h, dy):
        return pltpu.make_async_copy(
            w_hbm.at[pl.ds(dy * 1536, 1536), pl.ds(h * 256, 256)], wt.at[h, dy], w_sem.at[h, dy]
        )

    def wn_copies(ty):
        return [
            pltpu.make_async_copy(
                w_hbm.at[pl.ds(((2 - ty) * 3 + 2 - tx) * 512, 512)],
                wn.at[ty, :, pl.ds(tx * 512, 512)],
                wn_sem.at[ty, tx],
            )
            for tx in range(3)
        ]

    cot_copy = pltpu.make_async_copy(cot_hbm, cot, cot_sem)
    we_copy = pltpu.make_async_copy(we_hbm, we, we_sem)
    in_copies = [pltpu.make_async_copy(x_hbm.at[b], xin.at[b], in_sem.at[b]) for b in range(4)]
    for c in in_copies:
        c.start()
    for dy in range(3):
        w_copy(0, dy).start()
    cot_copy.start()
    we_copy.start()
    for dy in range(3):
        w_copy(1, dy).start()
    for ty in range(3):
        for c in wn_copies(ty):
            c.start()

    lax.fori_loop(1, 8, greet_outer, 0)
    lax.fori_loop(1, 16, greet_inner, 0)

    row = lax.broadcasted_iota(jnp.int32, (256, 256), 0)
    col = lax.broadcasted_iota(jnp.int32, (256, 256), 1)
    want = ((row // 4) % 4) * 64 + (row // 16) * 4 + row % 4
    perm[...] = jnp.where(want == col, 1.0, 0.0).astype(BF16)

    zero_row = jnp.zeros((16, 1536), BF16)
    for dst in (xs, hs):
        for b in range(4):
            dst[b, 0] = zero_row
            dst[b, 17] = zero_row
    gacc[...] = jnp.zeros_like(gacc)

    def spread(value, dst, b, r, first):
        n = value.shape[1]
        w = lax.broadcasted_iota(jnp.int32, (64, n), 0) % 16
        wide = value.astype(F32)
        left = jnp.where(w == 0, 0.0, pltpu.roll(wide, 1, 0)).astype(BF16)
        right = jnp.where(w == 15, 0.0, pltpu.roll(wide, 63, 0)).astype(BF16)
        for dx, v in ((0, left), (1, value), (2, right)):
            at = dx * 512 + first
            dst[b, pl.ds(1 + 4 * r, 4), :, at : at + n] = v.reshape(4, 16, n)


    for b in range(4):
        in_copies[b].wait()

        def prep(r, carry, b=b):
            v = xin[b, pl.ds(4 * r, 4)].reshape(64, 512)
            spread(jnp.maximum(v, jnp.zeros((), BF16)), xs, b, r, 0)
            return carry

        lax.fori_loop(0, 4, prep, 0)

    def tap_row(ref, dy):
        return ref[:, pl.ds(dy, 16)].reshape(1024, 1536)

    def conv_taps(h, dy, first):
        w_copy(h, dy).wait()
        part = nn(tap_row(xs, dy), wt[h, dy])
        if first:
            acc[...] = part
        else:
            acc[...] += part

    def finish_forward(h, total):
        pre = total.astype(BF16)
        hp[h] = pre
        ht[0, h] = nt(perm[...], jnp.maximum(pre, jnp.zeros((), BF16))).astype(BF16)

    def hidden_back(h, k):
        rows = pl.ds(pl.multiple_of(k * 512, 512), 512)
        chans = pl.ds(pl.multiple_of(h * 256, 256), 256)
        back = nt(cot[rows], we[chans])
        hg[h, rows] = jnp.where(hp[h, rows].astype(F32) > 0, back, 0.0).astype(BF16)

    def finish_back(h):
        ht[1, h] = nt(perm[...], hg[h]).astype(BF16)

    def produce(p, k):
        q = 2 * p + k
        h = q // 13
        j = q % 13

        @pl.when(j < 4)
        def _():
            g = nn(ht[0, h], cot[:, pl.ds(pl.multiple_of(j * 512, 512), 512)]) * (1.0 / 1024.0)
            gm[q] = g.astype(BF16).reshape(4, 4, 16, 512)

        @pl.when(j >= 4)
        def _():
            t = j - 4
            at = pl.multiple_of((t % 3) * 512, 512)
            g = nn(ht[1, h], xs[:, pl.ds(t // 3, 16), :, pl.ds(at, 512)].reshape(1024, 512)) * (1.0 / 1024.0)
            gm[q] = g.astype(BF16).reshape(4, 4, 16, 512)

    def ring(k, stage):
        if (k + stage) % 2 == 0:
            return z, ((z + 1) % 4) * 4 + y, ((z + 3) % 4) * 4 + y
        return y, z * 4 + (y + 1) % 4, z * 4 + (y + 3) % 4

    def opposite(k):
        return z * 4 + (y + 2) % 4 if k == 0 else ((z + 2) % 4) * 4 + y

    def block(p, k, at):
        q = 2 * p + k
        return gm.at[q, at] if k == 0 else gm.at[q, :, at]

    def remote(src, dst, send, recv, inner):
        return pltpu.make_async_remote_copy(
            src_ref=src, dst_ref=dst, send_sem=send, recv_sem=recv,
            device_id={"inner": inner}, device_id_type=MESH,
        )

    LO, HI = slice(0, 256), slice(256, 512)

    def copies1(p, k):
        at, nxt, prv = ring(k, 0)
        far = block(p, k, (at + 2) % 4)
        return (
            remote(far.at[:, :, LO], r1p.at[p, k], s1p, q1p.at[p, k], nxt),
            remote(far.at[:, :, HI], r1m.at[p, k], s1m, q1m.at[p, k], prv),
        )

    def copies2(p, k):
        at, nxt, prv = ring(k, 0)
        return (
            remote(block(p, k, (at + 1) % 4), r2p.at[p, k], s2p, q2p.at[p, k], nxt),
            remote(block(p, k, (at + 3) % 4), r2m.at[p, k], s2m, q2m.at[p, k], prv),
        )

    def copies3(p, k, last=False):
        at, nxt, prv = ring(k, 1)
        if last:
            nxt = prv = opposite(k)
        far = tb.at[p, k, (at + 2) % 4]
        return (
            remote(far.at[:, LO], r3p.at[p, k], s3p, q3p.at[p, k], nxt),
            remote(far.at[:, HI], r3m.at[p, k], s3m, q3m.at[p, k], prv),
        )

    def copies4(p, k):
        at, nxt, prv = ring(k, 1)
        return (
            remote(tb.at[p, k, (at + 1) % 4], r4p.at[p, k], s4p, q4p.at[p, k], nxt),
            remote(tb.at[p, k, (at + 3) % 4], r4m.at[p, k], s4m, q4m.at[p, k], prv),
        )

    def step1(p, k):
        for c in copies1(p, k):
            c.start()

    def step2(p, k):
        at, _, _ = ring(k, 0)
        fwd, bwd = copies1(p, k)
        out_fwd, out_bwd = copies2(p, k)
        near = block(p, k, (at + 1) % 4)
        fwd.wait_recv()
        near[:, :, LO] = (near[:, :, LO].astype(F32) + r1p[p, k].astype(F32)).astype(BF16)
        out_fwd.start()
        near = block(p, k, (at + 3) % 4)
        bwd.wait_recv()
        near[:, :, HI] = (near[:, :, HI].astype(F32) + r1m[p, k].astype(F32)).astype(BF16)
        out_bwd.start()

    def step3(p, k):
        at, _, _ = ring(k, 0)
        for c in copies2(p, k):
            c.wait_recv()
        mine = block(p, k, at)
        total = mine[...].astype(F32) + r2p[p, k].astype(F32) + r2m[p, k].astype(F32)
        tb[p, k] = total.astype(BF16)

        @pl.when(p < PAIRS - 1)
        def _():
            for c in copies3(p, k):
                c.start()

        @pl.when(p == PAIRS - 1)
        def _():
            for c in copies3(p, k, last=True) + copies4(p, k):
                c.start()

    def step4(p, k):
        @pl.when(p < PAIRS - 1)
        def _():
            at, _, _ = ring(k, 1)
            fwd, bwd = copies3(p, k)
            out_fwd, out_bwd = copies4(p, k)
            near = tb.at[p, k, (at + 1) % 4]
            fwd.wait_recv()
            near[:, LO] = (near[:, LO].astype(F32) + r3p[p, k].astype(F32)).astype(BF16)
            out_fwd.start()
            near = tb.at[p, k, (at + 3) % 4]
            bwd.wait_recv()
            near[:, HI] = (near[:, HI].astype(F32) + r3m[p, k].astype(F32)).astype(BF16)
            out_bwd.start()

    def x_copy(p, k, part, j, dest):
        return pltpu.make_async_remote_copy(
            src_ref=ub.at[p, k, part], dst_ref=rx.at[j, o], send_sem=sx, recv_sem=qx.at[j],
            device_id={"outer": dest}, device_id_type=MESH,
        )

    def step5(p, k):
        at, _, _ = ring(k, 1)
        q = 2 * p + k
        h = q // 13
        j = q % 13
        for c in copies4(p, k):
            c.wait_recv()
        tail = tb.at[p, k, at]

        @pl.when(p == PAIRS - 1)
        def _():
            for c in copies3(p, k, last=True):
                c.wait_recv()
            tail[:, LO] = (tail[:, LO].astype(F32) + r3p[p, k].astype(F32)).astype(BF16)
            tail[:, HI] = (tail[:, HI].astype(F32) + r3m[p, k].astype(F32)).astype(BF16)

        total = tail[...].astype(F32) + r4p[p, k].astype(F32) + r4m[p, k].astype(F32)
        for part in range(4):
            dest = h * 4 + part
            ub[p, k, part] = total[4 * part : 4 * part + 4]

            @pl.when(dest != o)
            def _():
                x_copy(p, k, part, j, dest).start()

            @pl.when(dest == o)
            def _():
                rx[j, o] = total[4 * part : 4 * part + 4]

    def step6(p, k):
        q = 2 * p + k
        j = q % 13

        @pl.when(q // 13 == o // 4)
        def _():
            pltpu.make_async_remote_copy(
                src_ref=rx.at[j, pl.ds(0, 7)], dst_ref=rx.at[j, pl.ds(0, 7)], send_sem=sx, recv_sem=qx.at[j],
                device_id={"outer": (o + 1) % 8}, device_id_type=MESH,
            ).wait_recv()
            kind = jnp.where(j < 4, 1, 0)
            vecs = [rx[j, a] for a in range(8)]
            for n, (a, b) in enumerate(GRAM):
                prod = vecs[a] * vecs[b]
                part = (prod[:, 0:128] + prod[:, 128:256]) + (prod[:, 256:384] + prod[:, 384:512])
                gacc[kind, n] = gacc[kind, n] + part

    for dy in range(3):
        w_copy(0, dy).wait()
    finish_forward(0, nn(tap_row(xs, 0), wt[0, 0]) + nn(tap_row(xs, 1), wt[0, 1]) + nn(tap_row(xs, 2), wt[0, 2]))
    cot_copy.wait()
    we_copy.wait()
    pl.semaphore_wait(barrier, 22)

    def image_rows(g, carry):
        b, r = g // 4, g % 4
        rows = pl.ds(pl.multiple_of(g * 64, 64), 64)
        for h in range(2):
            spread(hg[h, rows], hs, b, r, h * 256)
        return carry

    def input_piece(ty, m):
        part = nt(hs[pl.ds(2 * m, 2), pl.ds(ty, 16)].reshape(512, 1536), wn[ty])
        rows = pl.ds(pl.multiple_of(512 * m, 512), 512)
        if ty == 0:
            acc2[rows] = part
        elif ty == 1:
            acc2[rows] += part
        else:
            images = pl.ds(2 * m, 2)
            total = acc2[rows] + part
            kept = jnp.where(xin[images].reshape(512, 512).astype(F32) > 0, total, 0.0)
            ig[images] = kept.astype(BF16).reshape(2, 16, 16, 512)

    def input_work(p):
        @pl.when(p == INPUT_AT - 1)
        def _():
            lax.fori_loop(0, 16, image_rows, 0)

        for ty in range(3):

            @pl.when(jnp.logical_and(p >= INPUT_AT + 2 * ty, p < INPUT_AT + 2 * ty + 2))
            def _():
                m = p - (INPUT_AT + 2 * ty)

                @pl.when(m == 0)
                def _():
                    for c in wn_copies(ty):
                        c.wait()

                input_piece(ty, m)

    def iteration(p, carry):
        for k in range(2):

            @pl.when(p < PAIRS)
            def _():
                produce(p, k)
                step1(p, k)

        for lag, step in ((LAG2, step2), (LAG3, step3), (LAG4, step4), (LAG5, step5), (LAG6, step6)):

            @pl.when(jnp.logical_and(p >= lag, p < PAIRS + lag))
            def _():
                for k in range(2):
                    step(p - lag, k)

        @pl.when(jnp.logical_or(p < 2, jnp.logical_or(p == 6, p == 7)))
        def _():
            h = p // 6
            hidden_back(h, p % 2)

            @pl.when(p % 2 == 1)
            def _():
                finish_back(h)

        @pl.when(p == 2)
        def _():
            conv_taps(1, 0, True)

        @pl.when(jnp.logical_or(p == 3, p == 4))
        def _():
            conv_taps(1, p - 2, False)

            @pl.when(p == 4)
            def _():
                finish_forward(1, acc[...])

        input_work(p)
        return carry

    lax.fori_loop(0, PAIRS + LAG6, iteration, 0)

    lane = lax.broadcasted_iota(jnp.int32, (1, 128), 1)
    rows = []
    for kind in range(2):
        packed = jnp.zeros((1, 128), F32)
        for n in range(len(GRAM)):
            line = jnp.sum(gacc[kind, n], axis=0, keepdims=True)
            packed = jnp.where(lane == n, jnp.sum(line, axis=1, keepdims=True), packed)
        rows.append(packed)
    sub = lax.broadcasted_iota(jnp.int32, (2, 128), 0)
    mine = jnp.where(sub == 0, rows[0], rows[1])

    def exchange(axis, me, count, value, src, dst, send, recv):
        src[...] = value
        dst[me] = value

        def go(d, carry):
            pltpu.make_async_remote_copy(
                src_ref=src, dst_ref=dst.at[me], send_sem=send, recv_sem=recv,
                device_id={axis: (me + d) % count}, device_id_type=MESH,
            ).start()
            return carry

        lax.fori_loop(1, count, go, 0)
        got = dst.at[pl.ds(0, count - 1)]
        pltpu.make_async_remote_copy(
            src_ref=got, dst_ref=got, send_sem=send, recv_sem=recv,
            device_id={axis: (me + 1) % count}, device_id_type=MESH,
        ).wait_recv()
        total = dst[0]
        for n in range(1, count):
            total = total + dst[n]
        return total

    total = exchange("outer", o, 8, mine, stat.at[0], st1, ss1, qs1)
    total = exchange("inner", i, 16, total, stat.at[1], st2, ss2, qs2)
    gram = {ab: jnp.broadcast_to(total[:, n : n + 1], (2, 128)) for ab, n in GRAM_AT.items()}
    weights = adasum_weights(gram)

    for kind, count, out in ((0, 9, fin_conv), (1, 4, fin_exp)):
        coef = [jnp.broadcast_to(jnp.tile(w[kind : kind + 1], (1, 4)), (4, 512)) for w in weights]
        for t in range(count):
            j = t if kind == 1 else t + 4
            value = coef[0] * rx[j, 0]
            for a in range(1, 8):
                value = value + coef[a] * rx[j, a]
            out[:, t * 512 : (t + 1) * 512] = value

    def drain(ref, send):
        pltpu.make_async_remote_copy(
            src_ref=ref, dst_ref=ref, send_sem=send, recv_sem=qs1,
            device_id={"outer": (o + 1) % 8}, device_id_type=MESH,
        ).wait_send()

    for ref, send in (
        (r1p, s1p), (r1m, s1m), (r2p, s2p), (r2m, s2m), (r3p, s3p), (r3m, s3m), (r4p, s4p), (r4m, s4m),
        (rx.at[:, pl.ds(0, 7)], sx), (st1.at[pl.ds(0, 7)], ss1), (st2.at[pl.ds(0, 15)], ss2),
    ):
        drain(ref, send)


def update_kernel(
    ig, fin_conv, fin_exp, mom_conv, mom_exp, ig_out, conv_out, exp_out, new_conv, new_exp, out_sem
):
    copies = [pltpu.make_async_copy(ig, ig_out, out_sem.at[0])]
    copies[0].start()
    for at, fin, mom, new, out in (
        (1, fin_conv, mom_conv, new_conv, conv_out), (2, fin_exp, mom_exp, new_exp, exp_out),
    ):
        n = fin.shape[1]
        for s in range(4):
            new[0:1, s * n : (s + 1) * n] = MOMENTUM * mom[0:1, s * n : (s + 1) * n] + fin[s : s + 1, :]
        copies.append(pltpu.make_async_copy(new, out, out_sem.at[at]))
        copies[-1].start()
    for copy in copies:
        copy.wait()


def body(inputs, cotangent, conv_weight, expand_weight, conv_momentum, expand_momentum):
    images, height, across, channels = inputs.shape
    rows = images * height * across
    dma = pltpu.SemaphoreType.DMA
    vmem = pltpu.VMEM
    any_spec = pl.BlockSpec(memory_space=pl.ANY)
    vmem_spec = pl.BlockSpec(memory_space=pltpu.VMEM)
    input_grad, fin_conv, fin_exp = pl.pallas_call(
        kernel,
        out_shape=(vmem(inputs.shape, BF16), vmem((4, 4608), F32), vmem((4, 2048), F32)),
        in_specs=[any_spec] * 4,
        out_specs=(vmem_spec, vmem_spec, vmem_spec),
        scratch_shapes=[
            vmem((4, 16, 16, 512), BF16),
            vmem((4, 18, 16, 1536), BF16),
            vmem((2, 3, 1536, 256), BF16),
            vmem((3, 512, 1536), BF16),
            vmem((512, 2048), BF16),
            vmem((1024, 2048), BF16),
            vmem((1024, 256), F32),
            vmem((2, 1024, 256), BF16),
            vmem((2, 2, 256, 1024), BF16),
            vmem((2, 1024, 256), BF16),
            vmem((4, 18, 16, 1536), BF16),
            vmem((1024, 512), F32),
            vmem((256, 256), BF16),
            vmem((26, 4, 4, 16, 512), BF16),
            vmem((PAIRS, 2, 4, 16, 256), BF16),
            vmem((PAIRS, 2, 4, 16, 256), BF16),
            vmem((PAIRS, 2, 4, 16, 512), BF16),
            vmem((PAIRS, 2, 4, 16, 512), BF16),
            vmem((PAIRS, 2, 4, 16, 512), BF16),
            vmem((PAIRS, 2, 16, 256), BF16),
            vmem((PAIRS, 2, 16, 256), BF16),
            vmem((PAIRS, 2, 16, 512), BF16),
            vmem((PAIRS, 2, 16, 512), BF16),
            vmem((PAIRS, 2, 4, 4, 512), F32),
            vmem((13, 8, 4, 512), F32),
            vmem((2, len(GRAM), 4, 128), F32),
            vmem((2, 2, 128), F32),
            vmem((8, 2, 128), F32),
            vmem((16, 2, 128), F32),
            dma((4,)), dma((2, 3)), dma((3, 3)), dma, dma,
        ]
        + [dma((PAIRS, 2))] * 8
        + [dma((13,)), dma, dma]
        + [dma] * 11,
        compiler_params=pltpu.CompilerParams(
            collective_id=0, has_side_effects=True, vmem_limit_bytes=VMEM_LIMIT
        ),
    )(inputs, cotangent.reshape(rows, cotangent.shape[-1]), conv_weight, expand_weight)
    return pl.pallas_call(
        update_kernel,
        out_shape=(
            jax.ShapeDtypeStruct(inputs.shape, BF16),
            jax.ShapeDtypeStruct(conv_momentum.shape, F32),
            jax.ShapeDtypeStruct(expand_momentum.shape, F32),
        ),
        in_specs=[vmem_spec] * 5,
        out_specs=(any_spec,) * 3,
        scratch_shapes=[vmem(conv_momentum.shape, F32), vmem(expand_momentum.shape, F32), dma((3,))],
        compiler_params=pltpu.CompilerParams(vmem_limit_bytes=8 * 1024 * 1024),
    )(input_grad, fin_conv, fin_exp, conv_momentum, expand_momentum)


def solution(mesh):
    return jax.shard_map(
        body,
        mesh=mesh,
        in_specs=(
            P(("outer", "inner"), None, None, None),
            P(("outer", "inner"), None, None, None),
            P(),
            P(),
            P(("outer", "inner"), None),
            P(("outer", "inner"), None),
        ),
        out_specs=(
            P(("outer", "inner"), None, None, None),
            P(("outer", "inner"), None),
            P(("outer", "inner"), None),
        ),
        check_vma=False,
    )
```
